128 devices in a mesh: ctx: 16 (over x_hi, y, core), head: 8 (over z, x_lo).
Axes of the slice: x: 4 (x_hi: 2, x_lo: 2; x = x_hi * 2 + x_lo), y: 4, z: 4, core: 2. Of those that a mesh axis runs over, the one named last changes fastest.
Arguments:
- query: bfloat16 [16384, 4096], P(('ctx', 'head')), may hold values from -12 to 12
- key: bfloat16 [16384, 1024], P(('ctx', 'head')), may hold values from -4 to 4
- value: bfloat16 [16384, 1024], P(('ctx', 'head')), may hold values from -5 to 5
- d_out: bfloat16 [16384, 4096], P(('ctx', 'head')), may hold values from -5 to 5
- stretch_ids: int32 [32], replicated, may hold values from 0 to 31, as said below
Outputs:
- grad_query: bfloat16 [16384, 4096], P(('ctx', 'head'))
- grad_key: bfloat16 [16384, 1024], P(('ctx', 'head'))
- grad_value: bfloat16 [16384, 1024], P(('ctx', 'head'))
The draws below stay inside these ranges and needn't reach their ends.
Inputs may be any that keep to these rules, and one draw needn't show every extreme that they name: `stretch_ids`: a permutation in which slots 2r and 2r+1 hold blocks c and 31 - c for some c, in either order.
All inputs are finite; a program needn't handle non-finite values.
Results may differ from the reference program's by a relative error of at most 0.028.
Values may be sent and summed in bfloat16 or wider, within the bound.
A program may use at most 128 MiB of HBM per device.

```python
import jax
import jax.numpy as jnp
from jax import lax

QUERY_HEAD_COUNT = 32
KEY_VALUE_HEADS = 8
HEAD_SIZE = 128
WINDOW = 4
SEQUENCE_TOKENS = 16384
ROWS = 1024
STRETCH = 512
N_CTX = 16


def draw_query(key, part):
    value_rows = jnp.clip(jax.random.normal(jax.random.fold_in(key, 3), (SEQUENCE_TOKENS, QUERY_HEAD_COUNT * HEAD_SIZE)), -4.0, 4.0)
    return value_rows.astype(jnp.bfloat16)


def draw_key(key, part):
    value_rows = jnp.clip(jax.random.normal(jax.random.fold_in(key, 13), (SEQUENCE_TOKENS, KEY_VALUE_HEADS * HEAD_SIZE)), -4.0, 4.0)
    return value_rows.astype(jnp.bfloat16)


def draw_stretch_ids(key, part):
    order = jax.random.permutation(jax.random.fold_in(key, 21), N_CTX).astype(jnp.int32)
    flips = jax.random.randint(jax.random.fold_in(key, 22), (N_CTX,), 0, 2)
    first = jnp.where(flips == 1, 2 * N_CTX - 1 - order, order)
    second = 2 * N_CTX - 1 - first
    return jnp.stack((first, second), axis=1).reshape(2 * N_CTX).astype(jnp.int32)


def block_scale(key, dims, cuts, smallest, top_value):
    factor_of = 1.0
    for dim, blocks in cuts:
        draws = jax.random.uniform(jax.random.fold_in(jax.random.fold_in(key, 6), dim), (blocks,), jnp.float32, smallest / len(cuts), top_value / len(cuts))
        factor_of = factor_of * jnp.repeat(jnp.exp(draws), dims[dim] // blocks).reshape((-1,) + (1,) * (len(dims) - 1 - dim))
    return factor_of


def noise(rng, shape, scale, limit, split=(), kind=jnp.bfloat16):
    values = jax.random.normal(rng, shape, jnp.float32) * scale
    if len(split) > 0:
        values = block_scale(rng, shape, split, -0.22, 0.18) * values
    return jnp.clip(values, min=-limit, max=limit).astype(kind)


def setup_inputs(seed: int = 0) -> dict:
    key_of = jax.random.split(jax.random.key(seed), 6)
    return {
        "query": draw_query(jax.random.fold_in(key_of[5], 71), 0),
        "key": draw_key(jax.random.fold_in(key_of[5], 71), 0),
        "value": noise(key_of[2], (SEQUENCE_TOKENS, KEY_VALUE_HEADS * HEAD_SIZE), 1.0, 5.0, ((0, 128),)),
        "d_out": noise(key_of[3], (SEQUENCE_TOKENS, QUERY_HEAD_COUNT * HEAD_SIZE), 1.0, 5.0, ((0, 128),)),
        "stretch_ids": draw_stretch_ids(jax.random.fold_in(key_of[5], 71), 0),
    }


def reference(query, key, value, d_out, stretch_ids):
    rank_index = jnp.arange(SEQUENCE_TOKENS, dtype=jnp.int32)
    position = stretch_ids[rank_index // STRETCH].astype(jnp.int32) * STRETCH + rank_index % STRETCH
    scale = HEAD_SIZE ** -0.5
    group_width = QUERY_HEAD_COUNT // KEY_VALUE_HEADS
    query_heads = query.reshape(SEQUENCE_TOKENS, QUERY_HEAD_COUNT, HEAD_SIZE).transpose(1, 0, 2)
    grad_heads = d_out.reshape(SEQUENCE_TOKENS, QUERY_HEAD_COUNT, HEAD_SIZE).transpose(1, 0, 2)
    key_head_rows = jnp.repeat(key.reshape(SEQUENCE_TOKENS, KEY_VALUE_HEADS, HEAD_SIZE).transpose(1, 0, 2), group_width, axis=0)
    value_head_rows = jnp.repeat(value.reshape(SEQUENCE_TOKENS, KEY_VALUE_HEADS, HEAD_SIZE).transpose(1, 0, 2), group_width, axis=0)
    local = jnp.arange(ROWS, dtype=jnp.int32)
    offsets = jnp.arange(WINDOW, dtype=jnp.int32)

    def one_head(operands):
        q_all, g_all, k_all, v_all = operands

        def one_rank(carry, rank):
            grad_k_acc, grad_v_acc = carry
            q_rows = rank * ROWS + local
            k_rows = ((((rank - offsets) % N_CTX) * ROWS)[:, None] + local[None, :]).reshape(WINDOW * ROWS).astype(jnp.int32)
            q_one = q_all[q_rows]
            g_one = g_all[q_rows]
            k_one = k_all[k_rows]
            v_one = v_all[k_rows]
            visible = position[q_rows][:, None] >= position[k_rows][None, :]
            logits = jnp.dot(q_one, k_one.T, preferred_element_type=jnp.float32) * scale
            logits = jnp.where(visible, logits, -jnp.inf)
            top = jnp.max(logits, axis=1)
            log_total = top + jnp.log(jnp.sum(jnp.exp(logits - top[:, None]), axis=1))
            probs = jnp.exp(logits - log_total[:, None])
            probs_low = probs.astype(jnp.bfloat16)
            attn_out = jnp.dot(probs_low, v_one, preferred_element_type=jnp.float32)
            row_dot = jnp.sum(g_one.astype(jnp.float32) * attn_out, axis=1)
            value_gradient = jnp.dot(probs_low.T, g_one, preferred_element_type=jnp.float32)
            grad_p = jnp.dot(g_one, v_one.T, preferred_element_type=jnp.float32)
            grad_s = (probs * (grad_p - row_dot[:, None]) * scale).astype(jnp.bfloat16)
            grad_q = jnp.dot(grad_s, k_one, preferred_element_type=jnp.float32)
            key_gradient = jnp.dot(grad_s.T, q_one, preferred_element_type=jnp.float32)
            grad_k_acc = grad_k_acc.at[k_rows].add(key_gradient)
            grad_v_acc = grad_v_acc.at[k_rows].add(value_gradient)
            return (grad_k_acc, grad_v_acc), grad_q.astype(jnp.bfloat16)

        start = (jnp.zeros((SEQUENCE_TOKENS, HEAD_SIZE), jnp.float32), jnp.zeros((SEQUENCE_TOKENS, HEAD_SIZE), jnp.float32))
        (key_gradient, value_gradient), grad_q = lax.scan(one_rank, start, jnp.arange(N_CTX, dtype=jnp.int32))
        return grad_q.reshape(SEQUENCE_TOKENS, HEAD_SIZE), key_gradient, value_gradient

    grad_q, key_gradient, value_gradient = lax.map(one_head, (query_heads, grad_heads, key_head_rows, value_head_rows))
    key_gradient = jnp.sum(key_gradient.reshape(KEY_VALUE_HEADS, group_width, SEQUENCE_TOKENS, HEAD_SIZE), axis=1)
    value_gradient = jnp.sum(value_gradient.reshape(KEY_VALUE_HEADS, group_width, SEQUENCE_TOKENS, HEAD_SIZE), axis=1)
    out_q = grad_q.transpose(1, 0, 2).reshape(SEQUENCE_TOKENS, QUERY_HEAD_COUNT * HEAD_SIZE)
    key_output = key_gradient.transpose(1, 0, 2).reshape(SEQUENCE_TOKENS, KEY_VALUE_HEADS * HEAD_SIZE).astype(jnp.bfloat16)
    value_output = value_gradient.transpose(1, 0, 2).reshape(SEQUENCE_TOKENS, KEY_VALUE_HEADS * HEAD_SIZE).astype(jnp.bfloat16)
    return (out_q, key_output, value_output)
```

```python
import jax, functools
import jax.numpy as jnp
from jax import lax
from jax.experimental import pallas as pl
from jax.experimental.pallas import tpu as pltpu

D = 128
B = 512
C1 = (D ** -0.5) * 1.4426950408889634
SC = D ** -0.5
NT = (((1,), (1,)), ((), ()))

def nt(a, b):
    return lax.dot_general(a, b, NT, preferred_element_type=jnp.float32)

def nn(a, b):
    return lax.dot_general(a, b, (((1,), (0,)), ((), ())), preferred_element_type=jnp.float32)

def tile_of(i):
    k = i - 2 + jnp.where(i > 2, 1, 0)
    q = jnp.maximum(1, i - 4)
    return q, k

RC = 256

def pass_a(i, qi, ki, diag, qw, gw, kw, vw, p_s, dp_s, m_s, l_s, d_s):
    k = kw[ki]
    v = vw[ki]
    for r in range(B // RC):
        rs = pl.ds(r * RC, RC)
        q = qw[qi, rs, :]
        g = gw[qi, rs, :]
        s = nt(k, q)
        dp = nt(v, g)
        if diag:
            key = lax.broadcasted_iota(jnp.int32, (B, RC), 0)
            row = lax.broadcasted_iota(jnp.int32, (B, RC), 1) + r * RC
            s = jnp.where(row >= key, s, -1e30)
        m = jnp.max(s, axis=0, keepdims=True)
        p = jnp.exp2(s * C1 - m * C1)
        l_s[i, :, rs] = jnp.sum(p, axis=0, keepdims=True)
        d_s[i, :, rs] = jnp.sum(p * dp, axis=0, keepdims=True)
        m_s[i, :, rs] = m
        p_s[i, :, rs] = p.astype(jnp.bfloat16)
        dp_s[i, :, rs] = dp

def pass_b(i, qi, ki, qw, gw, kT, p_s, dp_s, c_s, e_s, dqT, dk, dv):
    for r in range(B // RC):
        rs = pl.ds(r * RC, RC)
        pn = p_s[i, :, rs].astype(jnp.float32) * c_s[i, :, rs]
        ds = (pn * (dp_s[i, :, rs] - e_s[i, :, rs])).astype(jnp.bfloat16)
        pn = pn.astype(jnp.bfloat16)
        dv[ki] += nn(pn, gw[qi, rs, :])
        dk[ki] += nn(ds, qw[qi, rs, :])
        dqT[qi, :, rs] += nn(kT[ki], ds)

def combine(es, m_s, l_s, d_s, c_s, e_s):
    neg = -3e38
    mlo = m_s[0]
    mhi = jnp.maximum(m_s[1], m_s[2])
    for s in range(3):
        mhi = jnp.maximum(mhi, m_s[3 + s])
        mx = m_s[6 + s]
        mlo = jnp.maximum(mlo, jnp.where(es[s], mx, neg))
        mhi = jnp.maximum(mhi, jnp.where(es[s], neg, mx))
    f = {}
    f[0] = jnp.exp2((m_s[0] - mlo) * C1)
    for t in range(1, 6):
        f[t] = jnp.exp2((m_s[t] - mhi) * C1)
    for s in range(3):
        f[6 + s] = jnp.exp2((m_s[6 + s] - jnp.where(es[s], mlo, mhi)) * C1)
    llo = f[0] * l_s[0]
    dlo = f[0] * d_s[0]
    lhi = f[1] * l_s[1]
    dhi = f[1] * d_s[1]
    for t in range(2, 6):
        lhi += f[t] * l_s[t]
        dhi += f[t] * d_s[t]
    for s in range(3):
        a = f[6 + s] * l_s[6 + s]
        b = f[6 + s] * d_s[6 + s]
        llo += jnp.where(es[s], a, 0.0)
        lhi += jnp.where(es[s], 0.0, a)
        dlo += jnp.where(es[s], b, 0.0)
        dhi += jnp.where(es[s], 0.0, b)
    rlo = 1.0 / llo
    rhi = 1.0 / lhi
    dlo = dlo * rlo
    dhi = dhi * rhi
    c_s[0] = f[0] * rlo
    e_s[0] = dlo
    for t in range(1, 6):
        c_s[t] = f[t] * rhi
        e_s[t] = dhi
    for s in range(3):
        c_s[6 + s] = f[6 + s] * jnp.where(es[s], rlo, rhi)
        e_s[6 + s] = jnp.where(es[s], dlo, dhi)

SCRATCH = dict(
    qw=pltpu.VMEM((5, B, D), jnp.bfloat16), gw=pltpu.VMEM((5, B, D), jnp.bfloat16),
    kw=pltpu.VMEM((8, B, D), jnp.bfloat16), vw=pltpu.VMEM((8, B, D), jnp.bfloat16),
    kT=pltpu.VMEM((8, D, B), jnp.bfloat16),
    p_s=pltpu.VMEM((9, B, B), jnp.bfloat16), dp_s=pltpu.VMEM((9, B, B), jnp.float32),
    m_s=pltpu.VMEM((9, 1, B), jnp.float32), l_s=pltpu.VMEM((9, 1, B), jnp.float32), d_s=pltpu.VMEM((9, 1, B), jnp.float32),
    c_s=pltpu.VMEM((9, 1, B), jnp.float32), e_s=pltpu.VMEM((9, 1, B), jnp.float32),
    dqT=pltpu.VMEM((5, D, B), jnp.float32), dk=pltpu.VMEM((8, B, D), jnp.float32), dv=pltpu.VMEM((8, B, D), jnp.float32))
NAMES = list(SCRATCH)

def load_kv(src, k, v, lowsel, e, S):
    for x, w in ((k, S['kw']), (v, S['vw'])):
        a, b = x[0:B], x[B:2 * B]
        lo = jnp.where(lowsel, b, a)
        hi = jnp.where(lowsel, a, b)
        if src == 0:
            w[0] = lo
            w[1] = hi
        else:
            w[1 + src] = lo
            w[4 + src] = jnp.where(e, lo, hi)
    for blk in ((0, 1) if src == 0 else (1 + src, 4 + src)):
        S['kT'][blk] = S['kw'][blk].T

def load_q(q, g, lowsel, es, S):
    for x, w in ((q, S['qw']), (g, S['gw'])):
        a, b = x[0:B], x[B:2 * B]
        lo = jnp.where(lowsel, b, a)
        hi = jnp.where(lowsel, a, b)
        w[0] = lo
        w[1] = hi
        for s in range(3):
            w[2 + s] = jnp.where(es[s], lo, hi)

def head_a(S):
    for i in (0, 1):
        pass_a(i, i, i, True, S['qw'], S['gw'], S['kw'], S['vw'], S['p_s'], S['dp_s'], S['m_s'], S['l_s'], S['d_s'])
    def step(i, _):
        qi, ki = tile_of(i)
        pass_a(i, qi, ki, False, S['qw'], S['gw'], S['kw'], S['vw'], S['p_s'], S['dp_s'], S['m_s'], S['l_s'], S['d_s'])
        return _
    lax.fori_loop(2, 9, step, 0)

def head_b(S):
    S['dqT'][...] = jnp.zeros_like(S['dqT'])
    for_b = functools.partial(pass_b, qw=S['qw'], gw=S['gw'], kT=S['kT'], p_s=S['p_s'], dp_s=S['dp_s'], c_s=S['c_s'], e_s=S['e_s'], dqT=S['dqT'], dk=S['dk'], dv=S['dv'])
    def step(i, _):
        qi, ki = tile_of(i)
        d = i < 2
        for_b(i, jnp.where(d, i, qi), jnp.where(d, i, ki))
        return _
    lax.fori_loop(0, 9, step, 0)

def finish_q(lowsel, es, S):
    dqT = S['dqT']
    lo = dqT[0]
    hi = dqT[1]
    for s in range(3):
        x = dqT[2 + s]
        lo = lo + jnp.where(es[s], x, 0.0)
        hi = hi + jnp.where(es[s], 0.0, x)
    lo = (lo * SC).T.astype(jnp.bfloat16)
    hi = (hi * SC).T.astype(jnp.bfloat16)
    return jnp.where(lowsel, hi, lo), jnp.where(lowsel, lo, hi)

def finish_kv(src, acc, scale, lowsel, e):
    if src == 0:
        lo, hi = acc[0], acc[1]
    else:
        x = acc[4 + src]
        lo = acc[1 + src] + jnp.where(e, x, 0.0)
        hi = jnp.where(e, 0.0, x)
    if scale != 1.0:
        lo, hi = lo * scale, hi * scale
    return jnp.where(lowsel, hi, lo), jnp.where(lowsel, lo, hi)
def kernel(info, q_ref, g_ref, k_ref, v_ref, dq_ref, gkv_ref, *scr):
    S = dict(zip(NAMES, scr))
    t = pl.program_id(0)
    low = [info[s] == 1 for s in range(4)]
    es = [info[4 + s] == 1 for s in range(3)]
    @pl.when(t == 0)
    def _():
        for s in range(4):
            load_kv(s, k_ref[s], v_ref[s], low[s], es[s - 1], S)
        S['dk'][...] = jnp.zeros_like(S['dk'])
        S['dv'][...] = jnp.zeros_like(S['dv'])
    load_q(q_ref[...], g_ref[...], low[0], es, S)
    head_a(S)
    combine(es, S['m_s'], S['l_s'], S['d_s'], S['c_s'], S['e_s'])
    head_b(S)
    a, b = finish_q(low[0], es, S)
    dq_ref[0:B] = a
    dq_ref[B:2 * B] = b
    @pl.when(t == 3)
    def _():
        for s in range(4):
            for n, (acc, scale) in enumerate(((S['dk'], SC), (S['dv'], 1.0))):
                a, b = finish_kv(s, acc, scale, low[s], es[s - 1])
                gkv_ref[s, n, 0:B] = a.astype(jnp.bfloat16)
                gkv_ref[s, n, B:2 * B] = b.astype(jnp.bfloat16)

def compute(info, q, g, k, v):
    return pl.pallas_call(
        kernel, grid=(4,),
        out_shape=(jax.ShapeDtypeStruct((1024, 512), jnp.bfloat16), jax.ShapeDtypeStruct((4, 2, 1024, 128), jnp.bfloat16)),
        in_specs=[pl.BlockSpec(memory_space=pltpu.SMEM), pl.BlockSpec((1024, 128), lambda t: (0, t)), pl.BlockSpec((1024, 128), lambda t: (0, t)),
                  pl.BlockSpec((4, 1024, 128), lambda t: (0, 0, 0)), pl.BlockSpec((4, 1024, 128), lambda t: (0, 0, 0))],
        out_specs=(pl.BlockSpec((1024, 128), lambda t: (0, t)), pl.BlockSpec((4, 2, 1024, 128), lambda t: (0, 0, 0, 0))),
        scratch_shapes=[SCRATCH[n] for n in NAMES],
        compiler_params=pltpu.CompilerParams(vmem_limit_bytes=60 << 20),
    )(info, q, g, k, v)

from jax.sharding import PartitionSpec as P

def shift(x, by):
    n = lax.axis_size("ctx")
    return lax.ppermute(x, "ctx", [(i, (i + by) % n) for i in range(n)])

def facts(stretch_ids):
    n = lax.axis_size("ctx")
    me = lax.axis_index("ctx")
    pairs = stretch_ids.reshape(-1, 2)
    ranks = (me - jnp.arange(4)) % n
    mine = pairs[ranks]
    low = (mine[:, 0] > mine[:, 1]).astype(jnp.int32)
    least = jnp.minimum(mine[:, 0], mine[:, 1])
    e = (least[0] > least[1:]).astype(jnp.int32)
    return jnp.concatenate([low, e, jnp.zeros((1,), jnp.int32)])

def body(query, key, value, d_out, stretch_ids):
    rows = query.shape[0]
    n = lax.axis_size("head")

    def a2a(x):
        w = x.shape[1] // n
        y = lax.all_to_all(x.reshape(rows, n, w), "head", split_axis=1, concat_axis=0, tiled=True)
        return y.reshape(rows * n, w)

    def back(x):
        w = x.shape[1]
        y = lax.all_to_all(x.reshape(rows * n, 1, w), "head", split_axis=0, concat_axis=1, tiled=True)
        return y.reshape(rows, n * w)

    info = facts(stretch_ids)
    kv = jnp.stack([a2a(key), a2a(value)])
    q, g = a2a(query), a2a(d_out)
    kvs = [kv] + [shift(kv, t) for t in (1, 2, 3)]
    k = jnp.stack([x[0] for x in kvs])
    v = jnp.stack([x[1] for x in kvs])
    dq, dkv = compute(info, q, g, k, v)
    total = dkv[0].astype(jnp.float32)
    for t in (1, 2, 3):
        total = total + shift(dkv[t], -t).astype(jnp.float32)
    total = total.astype(jnp.bfloat16)
    return back(dq), back(total[0]), back(total[1])

def solution(mesh):
    s = P(("ctx", "head"), None)
    return jax.shard_map(body, mesh=mesh, in_specs=(s, s, s, s, P()), out_specs=(s, s, s), check_vma=False)
```

```python
import functools

import jax
import jax.numpy as jnp
from jax import lax
from jax.experimental import pallas as pl
from jax.experimental.pallas import tpu as pltpu
from jax.sharding import PartitionSpec as P

HEADS = 4
KV_HEADS = 8
D = 128
B = 512
ROWS = 2 * B
WINDOW = 4
BF = jnp.bfloat16
F32 = jnp.float32
SCALE = D ** -0.5
LOG2E = 1.4426950408889634
C1 = SCALE * LOG2E
MESH = pl.DeviceIdType.MESH
TILES = 9


def nt(a, b):
    return lax.dot_general(a, b, (((1,), (1,)), ((), ())), preferred_element_type=F32)


def nn(a, b):
    return lax.dot_general(a, b, (((1,), (0,)), ((), ())), preferred_element_type=F32)


def kernel(
    info, query, key, value, d_out, gq, gk, gv,
    qg, kv, kw, vw, kt, p_s, dp_s, m_s, l_s, d_s, r_s, c_s, e_s, acc, dqt, dqo, cin, cout, fin,
    in_recv, in_send, kv_recv, kv_send, dq_recv, dq_send, c_recv, c_send, fin_recv, fin_send,
):
    c = lax.axis_index("ctx")
    hm = lax.axis_index("head")
    n_ctx = lax.axis_size("ctx")
    half = n_ctx // 2
    flip = c // half
    z, x = hm // 2, hm % 2

    def group_at(device):
        return device + flip * (1 - 2 * (device % 2))

    def ctx_peer(by):
        other = lax.rem(c + by + n_ctx, n_ctx)
        crossed = (other // half - flip) * (other // half - flip)
        return (other, hm + crossed * (1 - 2 * x))

    mine = group_at(hm)
    nxt, prv = ctx_peer(1), ctx_peer(-1)
    peers = []
    for dz, dx in ((1, 0), (3, 0), (0, 1), (2, 0), (1, 1), (3, 1), (2, 1)):
        pz = lax.rem(z + dz, 4)
        px = x + dx * (1 - 2 * x)
        peers.append(pz * 2 + px)

    low = [info[s] == 1 for s in range(WINDOW)]
    early = [None] + [info[3 + s] == 1 for s in range(1, WINDOW)]

    barrier = pltpu.get_barrier_semaphore()
    for j in peers:
        pl.semaphore_signal(barrier, inc=1, device_id=(c, j), device_id_type=MESH)
    for other in (nxt, prv):
        pl.semaphore_signal(barrier, inc=1, device_id=other, device_id_type=MESH)
    pl.semaphore_wait(barrier, 9)

    def remote(src, dst, ssem, rsem, dev):
        return pltpu.make_async_remote_copy(
            src_ref=src, dst_ref=dst, send_sem=ssem, recv_sem=rsem, device_id=dev, device_id_type=MESH)

    def cols(index):
        return pl.ds(pl.multiple_of(index * D, D), D)

    def rows(index):
        return pl.ds(pl.multiple_of(index * 128, 128), 128)

    for n, src in enumerate((key, value)):
        pltpu.make_async_copy(src.at[:, cols(mine)], kv.at[0, n, rows(hm)], in_recv.at[0]).start()
        for j in peers:
            remote(src.at[:, cols(group_at(j))], kv.at[0, n, rows(hm)], in_send.at[n], in_recv.at[0], (c, j)).start()

    def send_head(h, carry):
        for n, src in enumerate((query, d_out)):
            pltpu.make_async_copy(
                src.at[:, cols(mine * HEADS + h)], qg.at[h, n, rows(hm)], in_recv.at[1 + h]).start()
            for j in peers:
                remote(src.at[:, cols(group_at(j) * HEADS + h)], qg.at[h, n, rows(hm)],
                       in_send.at[2 + n], in_recv.at[1 + h], (c, j)).start()
        return carry

    lax.fori_loop(0, HEADS, send_head, 0)

    def arrived(buf, sem):
        pltpu.make_async_copy(buf, buf, sem).wait()

    def pick(cond, a, b):
        return jnp.where(cond, a, b)

    def take_kv(s):
        if s == 0:
            arrived(kv.at[0], in_recv.at[0])
        else:
            arrived(kv.at[s], kv_recv.at[s - 1])
        if s < WINDOW - 1:
            remote(kv.at[s], kv.at[s + 1], kv_send.at[s], kv_recv.at[s], nxt).start()
        for n, w in ((0, kw), (1, vw)):
            a, b = kv[s, n, 0:B], kv[s, n, B:ROWS]
            lo, hi = pick(low[s], b, a), pick(low[s], a, b)
            w[s, 0] = lo
            w[s, 1] = hi if s == 0 else pick(early[s], lo, hi)
        for b in (0, 1):
            kt[s, b] = kw[s, b].T

    def take_head(h):
        arrived(qg.at[h], in_recv.at[1 + h])
        for n in (0, 1):
            a, b = qg[h, n, 0:B], qg[h, n, B:ROWS]
            qg[h, n, 0:B] = pick(low[0], b, a)
            qg[h, n, B:ROWS] = pick(low[0], a, b)

    def block(h, n, b):
        return qg[h, n, b * B:(b + 1) * B]

    def mixed(h, n, s):
        return pick(early[s], block(h, n, 0), block(h, n, 1))

    def tile_a(h, t, k, v, q, g, diagonal):
        s = nt(k, q)
        dp = nt(v, g)
        if diagonal:
            seen = lax.broadcasted_iota(jnp.int32, (B, B), 1) >= lax.broadcasted_iota(jnp.int32, (B, B), 0)
            s = jnp.where(seen, s, -1e30)
        m = jnp.max(s, axis=0, keepdims=True)
        p = jnp.exp2(s * C1 - m * C1)
        l = jnp.sum(p, axis=0, keepdims=True)
        d = jnp.sum(p * dp, axis=0, keepdims=True)
        r = d / l
        m_s[t, pl.ds(h, 1)] = m
        l_s[t, pl.ds(h, 1)] = l
        d_s[t, pl.ds(h, 1)] = d
        r_s[t, pl.ds(h, 1)] = r
        p_s[h, t] = p.astype(BF)
        dp_s[h, t] = (dp - r).astype(BF)

    def own_a(h):
        tile_a(h, 2, kw[0, 0], vw[0, 0], block(h, 0, 1), block(h, 1, 1), False)
        tile_a(h, 0, kw[0, 0], vw[0, 0], block(h, 0, 0), block(h, 1, 0), True)
        tile_a(h, 1, kw[0, 1], vw[0, 1], block(h, 0, 1), block(h, 1, 1), True)

    def src_a(s, h):
        tile_a(h, 1 + 2 * s, kw[s, 0], vw[s, 0], block(h, 0, 1), block(h, 1, 1), False)
        tile_a(h, 2 + 2 * s, kw[s, 1], vw[s, 1], mixed(h, 0, s), mixed(h, 1, s), False)

    take_kv(0)
    take_kv(1)
    take_head(0)
    own_a(0)
    src_a(1, 0)
    take_kv(2)
    src_a(2, 0)
    take_head(1)
    own_a(1)
    src_a(1, 1)
    src_a(2, 1)
    take_kv(3)
    src_a(3, 0)
    src_a(3, 1)
    for h in (2, 3):
        take_head(h)
        own_a(h)
        for s in range(1, WINDOW):
            src_a(s, h)

    hi_tiles = [1, 2] + [1 + 2 * s for s in range(1, WINDOW)]
    m_lo, m_hi = m_s[0], m_s[1]
    for t in hi_tiles[1:]:
        m_hi = jnp.maximum(m_hi, m_s[t])
    for s in range(1, WINDOW):
        mx = m_s[2 + 2 * s]
        m_lo = jnp.maximum(m_lo, pick(early[s], mx, -3e38))
        m_hi = jnp.maximum(m_hi, pick(early[s], -3e38, mx))
    f = {0: jnp.exp2((m_s[0] - m_lo) * C1)}
    for t in hi_tiles:
        f[t] = jnp.exp2((m_s[t] - m_hi) * C1)
    l_lo, d_lo = f[0] * l_s[0], f[0] * d_s[0]
    l_hi = sum(f[t] * l_s[t] for t in hi_tiles)
    d_hi = sum(f[t] * d_s[t] for t in hi_tiles)
    for s in range(1, WINDOW):
        t = 2 + 2 * s
        f[t] = jnp.exp2((m_s[t] - pick(early[s], m_lo, m_hi)) * C1)
        a, b = f[t] * l_s[t], f[t] * d_s[t]
        l_lo += pick(early[s], a, 0.0)
        l_hi += pick(early[s], 0.0, a)
        d_lo += pick(early[s], b, 0.0)
        d_hi += pick(early[s], 0.0, b)
    i_lo, i_hi = 1.0 / l_lo, 1.0 / l_hi
    d_lo, d_hi = d_lo * i_lo, d_hi * i_hi
    c_s[0] = f[0] * i_lo
    e_s[0] = d_lo - r_s[0]
    for t in hi_tiles:
        c_s[t] = f[t] * i_hi
        e_s[t] = d_hi - r_s[t]
    for s in range(1, WINDOW):
        t = 2 + 2 * s
        c_s[t] = f[t] * pick(early[s], i_lo, i_hi)
        e_s[t] = pick(early[s], d_lo, d_hi) - r_s[t]

    def tile_b(h, t, k_t, q, g):
        pn = p_s[h, t].astype(F32) * c_s[t, pl.ds(h, 1)]
        ds = (pn * (dp_s[h, t].astype(F32) - e_s[t, pl.ds(h, 1)])).astype(BF)
        return nn(ds, q), nn(pn.astype(BF), g), nn(k_t, ds)

    def src_b(s, h, first):
        k0, v0, q0 = tile_b(h, 1 + 2 * s, kt[s, 0], block(h, 0, 1), block(h, 1, 1))
        k1, v1, q1 = tile_b(h, 2 + 2 * s, kt[s, 1], mixed(h, 0, s), mixed(h, 1, s))
        q_lo, q_hi = pick(early[s], q1, 0.0), q0 + pick(early[s], 0.0, q1)
        if first:
            acc[s, 0, 0], acc[s, 1, 0], acc[s, 0, 1], acc[s, 1, 1] = k0, v0, k1, v1
        else:
            acc[s, 0, 0] += k0
            acc[s, 1, 0] += v0
            acc[s, 0, 1] += k1
            acc[s, 1, 1] += v1
        if s == WINDOW - 1:
            dqt[h, 0], dqt[h, 1] = q_lo, q_hi
        else:
            dqt[h, 0] += q_lo
            dqt[h, 1] += q_hi

    def partial(s, n):
        unit = SCALE if n == 0 else 1.0
        if s == 0:
            return acc[0, n, 0] * unit, acc[0, n, 1] * unit
        lo, ex = acc[s, n, 0] * unit, acc[s, n, 1] * unit
        return lo + pick(early[s], ex, 0.0), pick(early[s], 0.0, ex)

    def pass_on(s):
        step = WINDOW - 1 - s
        if step > 0:
            arrived(cin.at[step - 1], c_recv.at[step - 1])
        for n in (0, 1):
            lo, hi = partial(s, n)
            if step > 0:
                lo = lo + cin[step - 1, n, 0:B].astype(F32)
                hi = hi + cin[step - 1, n, B:ROWS].astype(F32)
            cout[step, n, 0:B] = lo.astype(BF)
            cout[step, n, B:ROWS] = hi.astype(BF)
        remote(cout.at[step], cin.at[step], c_send.at[step], c_recv.at[step], prv).start()

    def source_b(s):
        for h in range(HEADS):
            src_b(s, h, h == 0)

    source_b(3)
    pass_on(3)
    source_b(2)
    source_b(1)
    pass_on(2)

    def out_rows(src, dst, col, ssem, rsem):
        pltpu.make_async_copy(src.at[rows(hm)], dst.at[:, cols(col)], rsem).start()
        for j in peers:
            remote(src.at[rows(j)], dst.at[:, cols(col)], ssem, rsem, (c, j)).start()

    def own_b(h, first):
        k2, v2, q2 = tile_b(h, 2, kt[0, 0], block(h, 0, 1), block(h, 1, 1))
        k0, v0, q0 = tile_b(h, 0, kt[0, 0], block(h, 0, 0), block(h, 1, 0))
        k1, v1, q1 = tile_b(h, 1, kt[0, 1], block(h, 0, 1), block(h, 1, 1))
        if first:
            acc[0, 0, 0], acc[0, 1, 0], acc[0, 0, 1], acc[0, 1, 1] = k0 + k2, v0 + v2, k1, v1
        else:
            acc[0, 0, 0] += k0 + k2
            acc[0, 1, 0] += v0 + v2
            acc[0, 0, 1] += k1
            acc[0, 1, 1] += v1
        lo = ((dqt[h, 0] + q0) * SCALE).T.astype(BF)
        hi = ((dqt[h, 1] + q1 + q2) * SCALE).T.astype(BF)
        dqo[h, 0:B] = pick(low[0], hi, lo)
        dqo[h, B:ROWS] = pick(low[0], lo, hi)
        out_rows(dqo.at[h], gq, mine * HEADS + h, dq_send.at[0], dq_recv.at[0])

    own_b(0, True)
    own_b(1, False)
    own_b(2, False)
    pass_on(1)
    own_b(3, False)

    arrived(cin.at[WINDOW - 2], c_recv.at[WINDOW - 2])
    for n, dst in ((0, gk), (1, gv)):
        lo, hi = partial(0, n)
        lo = (lo + cin[WINDOW - 2, n, 0:B].astype(F32)).astype(BF)
        hi = (hi + cin[WINDOW - 2, n, B:ROWS].astype(F32)).astype(BF)
        fin[n, 0:B] = pick(low[0], hi, lo)
        fin[n, B:ROWS] = pick(low[0], lo, hi)
        out_rows(fin.at[n], dst, mine, fin_send.at[n], fin_recv.at[n])

    sent = 128 - 128 // KV_HEADS
    for n, ref in enumerate((key, value, query, d_out)):
        arrived(ref.at[0:sent], in_send.at[n])
    for s in range(WINDOW - 1):
        arrived(kv.at[s], kv_send.at[s])
        arrived(cout.at[s], c_send.at[s])
    arrived(gq.at[0:sent], dq_send.at[0])
    arrived(gq, dq_recv.at[0])
    for n, ref in ((0, gk), (1, gv)):
        arrived(ref.at[0:sent], fin_send.at[n])
        arrived(ref, fin_recv.at[n])


def facts(stretch_ids):
    n = lax.axis_size("ctx")
    pairs = stretch_ids.reshape(-1, 2)
    own = pairs[(lax.axis_index("ctx") - jnp.arange(WINDOW)) % n]
    low = (own[:, 0] > own[:, 1]).astype(jnp.int32)
    least = jnp.minimum(own[:, 0], own[:, 1])
    early = (least[0] > least[1:]).astype(jnp.int32)
    return jnp.concatenate([low, early, jnp.zeros((1,), jnp.int32)])


def body(query, key, value, d_out, stretch_ids):
    anyspec = pl.BlockSpec(memory_space=pl.ANY)
    dma = pltpu.SemaphoreType.DMA
    stat = pltpu.VMEM((TILES, HEADS, B), F32)
    pair = (2, ROWS, D)
    return pl.pallas_call(
        kernel,
        out_shape=tuple(jax.ShapeDtypeStruct(a.shape, BF) for a in (query, key, value)),
        in_specs=[pl.BlockSpec(memory_space=pltpu.SMEM)] + [anyspec] * 4,
        out_specs=(anyspec,) * 3,
        scratch_shapes=[
            pltpu.VMEM((HEADS,) + pair, BF),
            pltpu.VMEM((WINDOW,) + pair, BF),
            pltpu.VMEM((WINDOW, 2, B, D), BF),
            pltpu.VMEM((WINDOW, 2, B, D), BF),
            pltpu.VMEM((WINDOW, 2, D, B), BF),
            pltpu.VMEM((HEADS, TILES, B, B), BF),
            pltpu.VMEM((HEADS, TILES, B, B), BF),
            stat, stat, stat, stat, stat, stat,
            pltpu.VMEM((WINDOW, 2, 2, B, D), F32),
            pltpu.VMEM((HEADS, 2, D, B), F32),
            pltpu.VMEM((HEADS, ROWS, D), BF),
            pltpu.VMEM((WINDOW - 1,) + pair, BF),
            pltpu.VMEM((WINDOW - 1,) + pair, BF),
            pltpu.VMEM(pair, BF),
            dma((1 + HEADS,)), dma((4,)), dma((WINDOW - 1,)), dma((WINDOW - 1,)),
            dma((1,)), dma((1,)), dma((WINDOW - 1,)), dma((WINDOW - 1,)), dma((2,)), dma((2,)),
        ],
        compiler_params=pltpu.CompilerParams(
            collective_id=0, has_side_effects=True, vmem_limit_bytes=67043328),
    )(facts(stretch_ids), query, key, value, d_out)


def solution(mesh):
    spec = P(("ctx", "head"), None)
    return jax.shard_map(
        body,
        mesh=mesh,
        in_specs=(spec, spec, spec, spec, P()),
        out_specs=(spec, spec, spec),
        check_vma=False,
    )
```

```python
import functools

import jax
import jax.numpy as jnp
from jax import lax
from jax.experimental import pallas as pl
from jax.experimental.pallas import tpu as pltpu
from jax.sharding import PartitionSpec as P

HEADS = 4
KV_HEADS = 8
D = 128
B = 512
ROWS = 2 * B
WINDOW = 4
BF = jnp.bfloat16
F32 = jnp.float32
SCALE = D ** -0.5
LOG2E = 1.4426950408889634
C1 = SCALE * LOG2E
MESH = pl.DeviceIdType.MESH
TILES = 9


def nt(a, b):
    return lax.dot_general(a, b, (((1,), (1,)), ((), ())), preferred_element_type=F32)


def nn(a, b):
    return lax.dot_general(a, b, (((1,), (0,)), ((), ())), preferred_element_type=F32)


def kernel(
    ids, query, key, value, d_out, gq, gk, gv,
    qg, kv, kw, vw, kt, p_s, dp_s, m_s, l_s, d_s, r_s, c_s, e_s, acc, dqt, dqo, cin, cout, fin,
    in_recv, in_send, kv_recv, kv_send, dq_recv, dq_send, c_recv, c_send, fin_recv, fin_send,
):
    c = lax.axis_index("ctx")
    hm = lax.axis_index("head")
    n_ctx = lax.axis_size("ctx")
    half = n_ctx // 2
    flip = c // half
    z, x = hm // 2, hm % 2

    def group_at(device):
        return device + flip * (1 - 2 * (device % 2))

    def ctx_peer(by):
        other = lax.rem(c + by + n_ctx, n_ctx)
        crossed = (other // half - flip) * (other // half - flip)
        return (other, hm + crossed * (1 - 2 * x))

    mine = group_at(hm)
    nxt, prv = ctx_peer(1), ctx_peer(-1)
    peers = []
    for dz, dx in ((1, 0), (3, 0), (0, 1), (2, 0), (1, 1), (3, 1), (2, 1)):
        pz = lax.rem(z + dz, 4)
        px = x + dx * (1 - 2 * x)
        peers.append(pz * 2 + px)

    ranks = [lax.rem(c - s + n_ctx, n_ctx) for s in range(WINDOW)]
    pairs = [(ids[2 * r], ids[2 * r + 1]) for r in ranks]
    low = [a > b for a, b in pairs]
    least = [jnp.minimum(a, b) for a, b in pairs]
    early = [None] + [least[0] > least[s] for s in range(1, WINDOW)]

    barrier = pltpu.get_barrier_semaphore()
    for j in peers:
        pl.semaphore_signal(barrier, inc=1, device_id=(c, j), device_id_type=MESH)
    for other in (nxt, prv):
        pl.semaphore_signal(barrier, inc=1, device_id=other, device_id_type=MESH)
    pl.semaphore_wait(barrier, 9)

    def remote(src, dst, ssem, rsem, dev):
        return pltpu.make_async_remote_copy(
            src_ref=src, dst_ref=dst, send_sem=ssem, recv_sem=rsem, device_id=dev, device_id_type=MESH)

    def cols(index):
        return pl.ds(pl.multiple_of(index * D, D), D)

    def rows(index):
        return pl.ds(pl.multiple_of(index * 128, 128), 128)

    for n, src in enumerate((key, value)):
        pltpu.make_async_copy(src.at[:, cols(mine)], kv.at[0, n, rows(hm)], in_recv.at[0]).start()
        for j in peers:
            remote(src.at[:, cols(group_at(j))], kv.at[0, n, rows(hm)], in_send.at[n], in_recv.at[0], (c, j)).start()

    def send_head(h, carry):
        for n, src in enumerate((query, d_out)):
            pltpu.make_async_copy(
                src.at[:, cols(mine * HEADS + h)], qg.at[h, n, rows(hm)], in_recv.at[1 + h]).start()
            for j in peers:
                remote(src.at[:, cols(group_at(j) * HEADS + h)], qg.at[h, n, rows(hm)],
                       in_send.at[2 + n], in_recv.at[1 + h], (c, j)).start()
        return carry

    lax.fori_loop(0, HEADS, send_head, 0)

    def arrived(buf, sem):
        pltpu.make_async_copy(buf, buf, sem).wait()

    def pick(cond, a, b):
        return jnp.where(cond, a, b)

    def relay(s):
        if s == 0:
            arrived(kv.at[0], in_recv.at[0])
        else:
            arrived(kv.at[s], kv_recv.at[s - 1])
        if s < WINDOW - 1:
            remote(kv.at[s], kv.at[s + 1], kv_send.at[s], kv_recv.at[s], nxt).start()

    def prep(s):
        for n, w in ((0, kw), (1, vw)):
            a, b = kv[s, n, 0:B], kv[s, n, B:ROWS]
            lo, hi = pick(low[s], b, a), pick(low[s], a, b)
            w[s, 0] = lo
            w[s, 1] = hi if s == 0 else pick(early[s], lo, hi)
        for b in (0, 1):
            kt[s, b] = kw[s, b].T

    def take_head(h):
        arrived(qg.at[h], in_recv.at[1 + h])
        for n in (0, 1):
            a, b = qg[h, n, 0:B], qg[h, n, B:ROWS]
            qg[h, n, 0:B] = pick(low[0], b, a)
            qg[h, n, B:ROWS] = pick(low[0], a, b)

    def block(h, n, b):
        return qg[h, n, b * B:(b + 1) * B]

    def mixed(h, n, s):
        return pick(early[s], block(h, n, 0), block(h, n, 1))

    half_b = B // 2

    def stats(h, t, cs, parts):
        m = functools.reduce(jnp.maximum, [jnp.max(x, axis=0, keepdims=True) for _, x, _ in parts])
        ps = [jnp.exp2(x * C1 - m * C1) for _, x, _ in parts]
        l = sum(jnp.sum(p, axis=0, keepdims=True) for p in ps)
        d = sum(jnp.sum(p * y, axis=0, keepdims=True) for p, (_, _, y) in zip(ps, parts))
        r = d / l
        m_s[t, pl.ds(h, 1), cs] = m
        l_s[t, pl.ds(h, 1), cs] = l
        d_s[t, pl.ds(h, 1), cs] = d
        r_s[t, pl.ds(h, 1), cs] = r
        for p, (rs, _, y) in zip(ps, parts):
            p_s[h, t, rs, cs] = p.astype(BF)
            dp_s[h, t, rs, cs] = (y - r).astype(BF)

    whole, first, second = slice(0, B), slice(0, half_b), slice(half_b, B)

    def tile_a(h, t, k, v, q, g, diagonal):
        if not diagonal:
            stats(h, t, whole, [(whole, nt(k, q), nt(v, g))])
            return
        seen = (lax.broadcasted_iota(jnp.int32, (half_b, half_b), 1)
                >= lax.broadcasted_iota(jnp.int32, (half_b, half_b), 0))
        s0, y0 = nt(k[first], q), nt(v[first], g)
        s1, y1 = nt(k[second], q[second]), nt(v[second], g[second])
        stats(h, t, first, [(first, jnp.where(seen, s0[:, first], -1e30), y0[:, first])])
        stats(h, t, second, [(first, s0[:, second], y0[:, second]), (second, jnp.where(seen, s1, -1e30), y1)])

    def own_a(h):
        tile_a(h, 2, kw[0, 0], vw[0, 0], block(h, 0, 1), block(h, 1, 1), False)
        tile_a(h, 0, kw[0, 0], vw[0, 0], block(h, 0, 0), block(h, 1, 0), True)
        tile_a(h, 1, kw[0, 1], vw[0, 1], block(h, 0, 1), block(h, 1, 1), True)

    def src_a(s, h):
        tile_a(h, 1 + 2 * s, kw[s, 0], vw[s, 0], block(h, 0, 1), block(h, 1, 1), False)
        tile_a(h, 2 + 2 * s, kw[s, 1], vw[s, 1], mixed(h, 0, s), mixed(h, 1, s), False)

    def totals(hs):
        hi_tiles = [1, 2] + [1 + 2 * s for s in range(1, WINDOW)]
        m_lo, m_hi = m_s[0, hs], m_s[1, hs]
        for t in hi_tiles[1:]:
            m_hi = jnp.maximum(m_hi, m_s[t, hs])
        for s in range(1, WINDOW):
            mx = m_s[2 + 2 * s, hs]
            m_lo = jnp.maximum(m_lo, pick(early[s], mx, -3e38))
            m_hi = jnp.maximum(m_hi, pick(early[s], -3e38, mx))
        f = {0: jnp.exp2((m_s[0, hs] - m_lo) * C1)}
        for t in hi_tiles:
            f[t] = jnp.exp2((m_s[t, hs] - m_hi) * C1)
        l_lo, d_lo = f[0] * l_s[0, hs], f[0] * d_s[0, hs]
        l_hi = sum(f[t] * l_s[t, hs] for t in hi_tiles)
        d_hi = sum(f[t] * d_s[t, hs] for t in hi_tiles)
        for s in range(1, WINDOW):
            t = 2 + 2 * s
            f[t] = jnp.exp2((m_s[t, hs] - pick(early[s], m_lo, m_hi)) * C1)
            a, b = f[t] * l_s[t, hs], f[t] * d_s[t, hs]
            l_lo += pick(early[s], a, 0.0)
            l_hi += pick(early[s], 0.0, a)
            d_lo += pick(early[s], b, 0.0)
            d_hi += pick(early[s], 0.0, b)
        i_lo, i_hi = 1.0 / l_lo, 1.0 / l_hi
        d_lo, d_hi = d_lo * i_lo, d_hi * i_hi
        c_s[0, hs] = f[0] * i_lo
        e_s[0, hs] = d_lo - r_s[0, hs]
        for t in hi_tiles:
            c_s[t, hs] = f[t] * i_hi
            e_s[t, hs] = d_hi - r_s[t, hs]
        for s in range(1, WINDOW):
            t = 2 + 2 * s
            c_s[t, hs] = f[t] * pick(early[s], i_lo, i_hi)
            e_s[t, hs] = pick(early[s], d_lo, d_hi) - r_s[t, hs]

    acc[...] = jnp.zeros_like(acc)
    dqt[...] = jnp.zeros_like(dqt)
    core = c % 2
    relay(0)
    prep(0)
    relay(1)
    prep(1)

    def head_step(h, carry):
        take_head(h)
        own_a(h)
        src_a(1, h)

        @pl.when(h + core == 1)
        def _():
            relay(2)

        @pl.when(h == 1)
        def _():
            prep(2)
            src_a(2, 0)
            src_a(2, 1)

        return carry

    lax.fori_loop(0, 2, head_step, 0)
    take_head(2)
    own_a(2)
    src_a(1, 2)
    src_a(2, 2)
    relay(3)
    prep(3)

    def far_step(h, carry):
        src_a(3, h)
        return carry

    lax.fori_loop(0, 3, far_step, 0)

    def weights(h, t, rs, cs):
        pn = p_s[h, t, rs, cs].astype(F32) * c_s[t, pl.ds(h, 1), cs]
        ds = (pn * (dp_s[h, t, rs, cs].astype(F32) - e_s[t, pl.ds(h, 1), cs])).astype(BF)
        return pn.astype(BF), ds

    def tile_b(h, t, k_t, q, g):
        p, ds = weights(h, t, whole, whole)
        return nn(ds, q), nn(p, g), nn(k_t, ds)

    def src_b(s, hs):
        ks, vs = [], []
        for h in hs:
            k0, v0, q0 = tile_b(h, 1 + 2 * s, kt[s, 0], block(h, 0, 1), block(h, 1, 1))
            k1, v1, q1 = tile_b(h, 2 + 2 * s, kt[s, 1], mixed(h, 0, s), mixed(h, 1, s))
            dqt[h, 0] += pick(early[s], q1, 0.0)
            dqt[h, 1] += q0 + pick(early[s], 0.0, q1)
            ks.append((k0, k1))
            vs.append((v0, v1))
        for b in (0, 1):
            acc[s, 0, b] += sum(k[b] for k in ks)
            acc[s, 1, b] += sum(v[b] for v in vs)

    def partial(s, n):
        unit = SCALE if n == 0 else 1.0
        if s == 0:
            return acc[0, n, 0] * unit, acc[0, n, 1] * unit
        lo, ex = acc[s, n, 0] * unit, acc[s, n, 1] * unit
        return lo + pick(early[s], ex, 0.0), pick(early[s], 0.0, ex)

    def pass_on(s):
        step = WINDOW - 1 - s
        for n in (1, 0):
            lo, hi = partial(s, n)
            if step > 0:
                arrived(cin.at[step - 1, n], c_recv.at[step - 1, n])
                lo = lo + cin[step - 1, n, 0:B].astype(F32)
                hi = hi + cin[step - 1, n, B:ROWS].astype(F32)
            cout[step, n, 0:B] = lo.astype(BF)
            cout[step, n, B:ROWS] = hi.astype(BF)
            remote(cout.at[step, n], cin.at[step, n], c_send.at[step], c_recv.at[step, n], prv).start()

    def out_rows(src, dst, col, ssem, rsem):
        pltpu.make_async_copy(src.at[rows(hm)], dst.at[:, cols(col)], rsem).start()
        for j in peers:
            remote(src.at[rows(j)], dst.at[:, cols(col)], ssem, rsem, (c, j)).start()

    def diag_b(h, t, k_t, q, g):
        p0, ds0 = weights(h, t, first, first)
        p1, ds1 = weights(h, t, whole, second)
        return ((nn(ds0, q[first]), nn(ds1, q[second])), (nn(p0, g[first]), nn(p1, g[second])),
                (nn(k_t[:, first], ds0), nn(k_t, ds1)))

    def own_b(h):
        k2, v2, q2 = tile_b(h, 2, kt[0, 0], block(h, 0, 1), block(h, 1, 1))
        dk0, dv0, q0 = diag_b(h, 0, kt[0, 0], block(h, 0, 0), block(h, 1, 0))
        dk1, dv1, q1 = diag_b(h, 1, kt[0, 1], block(h, 0, 1), block(h, 1, 1))
        for n, full, d0, d1 in ((0, k2, dk0, dk1), (1, v2, dv0, dv1)):
            acc[0, n, 0] += full + d0[1]
            acc[0, n, 0, first] += d0[0]
            acc[0, n, 1] += d1[1]
            acc[0, n, 1, first] += d1[0]
        for cs, a, b in ((first, q0[0], q1[0]), (second, q0[1], q1[1])):
            lo = ((dqt[h, 0, :, cs] + a) * SCALE).T.astype(BF)
            hi = ((dqt[h, 1, :, cs] + b + q2[:, cs]) * SCALE).T.astype(BF)
            dqo[h, cs] = pick(low[0], hi, lo)
            dqo[h, slice(cs.start + B, cs.stop + B)] = pick(low[0], lo, hi)
        out_rows(dqo.at[h], gq, mine * HEADS + h, dq_send.at[0], dq_recv.at[0])

    totals(slice(0, 3))

    def far_b(h, carry):
        src_b(3, (h,))
        return carry

    lax.fori_loop(0, 3, far_b, 0)
    take_head(3)
    own_a(3)
    for s in range(1, WINDOW):
        src_a(s, 3)
    totals(slice(3, 4))
    src_b(3, (3,))
    pass_on(3)

    def near_b(i, carry):
        src_b(2, (2 * i, 2 * i + 1))
        return carry

    lax.fori_loop(0, 2, near_b, 0)

    @pl.when(core == 0)
    def _():
        pass_on(2)

    def last_b(h, carry):
        src_b(1, (h,))
        own_b(h)

        @pl.when(h * core == 1)
        def _():
            pass_on(2)

        return carry

    lax.fori_loop(0, HEADS, last_b, 0)
    pass_on(1)

    for n, dst in ((1, gv), (0, gk)):
        lo, hi = partial(0, n)
        arrived(cin.at[WINDOW - 2, n], c_recv.at[WINDOW - 2, n])
        lo = (lo + cin[WINDOW - 2, n, 0:B].astype(F32)).astype(BF)
        hi = (hi + cin[WINDOW - 2, n, B:ROWS].astype(F32)).astype(BF)
        fin[n, 0:B] = pick(low[0], hi, lo)
        fin[n, B:ROWS] = pick(low[0], lo, hi)
        out_rows(fin.at[n], dst, mine, fin_send.at[n], fin_recv.at[n])

    sent = 128 - 128 // KV_HEADS
    for n, ref in enumerate((key, value, query, d_out)):
        arrived(ref.at[0:sent], in_send.at[n])
    for s in range(WINDOW - 1):
        arrived(kv.at[s], kv_send.at[s])
        arrived(cout.at[s], c_send.at[s])
    arrived(gq.at[0:sent], dq_send.at[0])
    arrived(gq, dq_recv.at[0])
    for n, ref in ((0, gk), (1, gv)):
        arrived(ref.at[0:sent], fin_send.at[n])
        arrived(ref, fin_recv.at[n])


def land(a, b, c, x, y, z):
    x[...] = a[...]
    y[...] = b[...]
    z[...] = c[...]


def body(query, key, value, d_out, stretch_ids):
    anyspec = pl.BlockSpec(memory_space=pl.ANY)
    dma = pltpu.SemaphoreType.DMA
    stat = pltpu.VMEM((TILES, HEADS, B), F32)
    pair = (2, ROWS, D)
    outs = pl.pallas_call(
        kernel,
        out_shape=tuple(jax.ShapeDtypeStruct(a.shape, BF) for a in (query, key, value)),
        in_specs=[pl.BlockSpec(memory_space=pltpu.SMEM)] + [anyspec] * 4,
        out_specs=(anyspec,) * 3,
        scratch_shapes=[
            pltpu.VMEM((HEADS,) + pair, BF),
            pltpu.VMEM((WINDOW,) + pair, BF),
            pltpu.VMEM((WINDOW, 2, B, D), BF),
            pltpu.VMEM((WINDOW, 2, B, D), BF),
            pltpu.VMEM((WINDOW, 2, D, B), BF),
            pltpu.VMEM((HEADS, TILES, B, B), BF),
            pltpu.VMEM((HEADS, TILES, B, B), BF),
            stat, stat, stat, stat, stat, stat,
            pltpu.VMEM((WINDOW, 2, 2, B, D), F32),
            pltpu.VMEM((HEADS, 2, D, B), F32),
            pltpu.VMEM((HEADS, ROWS, D), BF),
            pltpu.VMEM((WINDOW - 1,) + pair, BF),
            pltpu.VMEM((WINDOW - 1,) + pair, BF),
            pltpu.VMEM(pair, BF),
            dma((1 + HEADS,)), dma((4,)), dma((WINDOW - 1,)), dma((WINDOW - 1,)),
            dma((1,)), dma((1,)), dma((WINDOW - 1, 2)), dma((WINDOW - 1,)), dma((2,)), dma((2,)),
        ],
        compiler_params=pltpu.CompilerParams(
            collective_id=0, has_side_effects=True, vmem_limit_bytes=67043328),
    )(stretch_ids, query, key, value, d_out)
    blocks = [pl.BlockSpec((a.shape[0] // 4, a.shape[1]), lambda i: (i, 0)) for a in outs]
    return pl.pallas_call(
        land, grid=(4,), in_specs=blocks, out_specs=tuple(blocks),
        out_shape=tuple(jax.ShapeDtypeStruct(a.shape, BF) for a in outs))(*outs)


def solution(mesh):
    spec = P(("ctx", "head"), None)
    return jax.shard_map(
        body,
        mesh=mesh,
        in_specs=(spec, spec, spec, spec, P()),
        out_specs=(spec, spec, spec),
        check_vma=False,
    )
```

```python
import functools

import jax
import jax.numpy as jnp
from jax import lax
from jax.experimental import pallas as pl
from jax.experimental.pallas import tpu as pltpu
from jax.sharding import PartitionSpec as P

HEADS = 4
KV_HEADS = 8
D = 128
B = 512
ROWS = 2 * B
WINDOW = 4
BF = jnp.bfloat16
F32 = jnp.float32
SCALE = D ** -0.5
LOG2E = 1.4426950408889634
C1 = SCALE * LOG2E
MESH = pl.DeviceIdType.MESH
TILES = 9


def nt(a, b):
    return lax.dot_general(a, b, (((1,), (1,)), ((), ())), preferred_element_type=F32)


def nn(a, b):
    return lax.dot_general(a, b, (((1,), (0,)), ((), ())), preferred_element_type=F32)


def kernel(
    ids, query, key, value, d_out, gq, gk, gv,
    qg, kv, kw, vw, kt, p_s, dp_s, m_s, l_s, d_s, c_s, elo_s, ehi_s, r_s, mid, acc, dqt, cin,
    in_recv, in_send, kv_recv, kv_send, dq_recv, dq_send, c_recv, c_send, fin_recv, fin_send,
):
    c = lax.axis_index("ctx")
    hm = lax.axis_index("head")
    n_ctx = lax.axis_size("ctx")
    half = n_ctx // 2
    flip = c // half
    z, x = hm // 2, hm % 2

    def group_at(device):
        return device + flip * (1 - 2 * (device % 2))

    def ctx_peer(by):
        other = lax.rem(c + by + n_ctx, n_ctx)
        crossed = (other // half - flip) * (other // half - flip)
        return (other, hm + crossed * (1 - 2 * x))

    mine = group_at(hm)
    nxt, prv = ctx_peer(1), ctx_peer(-1)
    peers = []
    for dz, dx in ((1, 0), (3, 0), (0, 1), (2, 0), (1, 1), (3, 1), (2, 1)):
        pz = lax.rem(z + dz, 4)
        px = x + dx * (1 - 2 * x)
        peers.append(pz * 2 + px)

    ranks = [lax.rem(c - s + n_ctx, n_ctx) for s in range(WINDOW)]
    pairs = [(ids[2 * r], ids[2 * r + 1]) for r in ranks]
    low = [a > b for a, b in pairs]
    least = [jnp.minimum(a, b) for a, b in pairs]
    early = [None] + [least[0] > least[s] for s in range(1, WINDOW)]

    barrier = pltpu.get_barrier_semaphore()
    for j in peers:
        pl.semaphore_signal(barrier, inc=1, device_id=(c, j), device_id_type=MESH)
    for other in (nxt, prv):
        pl.semaphore_signal(barrier, inc=1, device_id=other, device_id_type=MESH)
    pl.semaphore_wait(barrier, 9)

    def remote(src, dst, ssem, rsem, dev):
        return pltpu.make_async_remote_copy(
            src_ref=src, dst_ref=dst, send_sem=ssem, recv_sem=rsem, device_id=dev, device_id_type=MESH)

    def cols(index):
        return pl.ds(pl.multiple_of(index * D, D), D)

    def rows(index):
        return pl.ds(pl.multiple_of(index * 128, 128), 128)

    for n, src in enumerate((key, value)):
        pltpu.make_async_copy(src.at[:, cols(mine)], kv.at[0, n, rows(hm)], in_recv.at[0]).start()
        for j in peers:
            remote(src.at[:, cols(group_at(j))], kv.at[0, n, rows(hm)], in_send.at[n], in_recv.at[0], (c, j)).start()

    def send_head(h, carry):
        for n, src in enumerate((query, d_out)):
            pltpu.make_async_copy(
                src.at[:, cols(mine * HEADS + h)], qg.at[h, n, rows(hm)], in_recv.at[1 + h]).start()
            for j in peers:
                remote(src.at[:, cols(group_at(j) * HEADS + h)], qg.at[h, n, rows(hm)],
                       in_send.at[2 + n], in_recv.at[1 + h], (c, j)).start()
        return carry

    lax.fori_loop(0, HEADS, send_head, 0)

    def arrived(buf, sem):
        pltpu.make_async_copy(buf, buf, sem).wait()

    def pick(cond, a, b):
        return jnp.where(cond, a, b)

    def relay(s):
        if s == 0:
            arrived(kv.at[0], in_recv.at[0])
        else:
            arrived(kv.at[s], kv_recv.at[s - 1])
        if s < WINDOW - 1:
            remote(kv.at[s], kv.at[s + 1], kv_send.at[s], kv_recv.at[s], nxt).start()

    def prep(s):
        for n, w in ((0, kw), (1, vw)):
            a, b = kv[s, n, 0:B], kv[s, n, B:ROWS]
            lo, hi = pick(low[s], b, a), pick(low[s], a, b)
            w[s, 0] = lo
            w[s, 1] = hi if s == 0 else pick(early[s], lo, hi)
        for b in (0, 1):
            kt[s, b] = kw[s, b].T

    def take_head(h):
        arrived(qg.at[h], in_recv.at[1 + h])
        for n in (0, 1):
            a, b = qg[h, n, 0:B], qg[h, n, B:ROWS]
            qg[h, n, 0:B] = pick(low[0], b, a)
            qg[h, n, B:ROWS] = pick(low[0], a, b)
        for b in (0, 1):
            r_s[h, b] = nt(mid[...], block(h, 1, b))

    def block(h, n, b):
        return qg[h, n, b * B:(b + 1) * B]

    def mixed(h, n, s):
        return pick(early[s], block(h, n, 0), block(h, n, 1))

    half_b = B // 2

    def stats(h, t, cs, r, parts):
        m = functools.reduce(jnp.maximum, [jnp.max(x, axis=0, keepdims=True) for _, x, _ in parts])
        l, d = 0.0, 0.0
        for rs, x, y in parts:
            p = jnp.exp2(x * C1 - m * C1)
            y = y - r[:, cs]
            l = l + jnp.sum(p, axis=0, keepdims=True)
            d = d + jnp.sum(p * y, axis=0, keepdims=True)
            p_s[h, t, rs, cs] = p.astype(BF)
            dp_s[h, t, rs, cs] = y.astype(BF)
        m_s[h, t, :, cs] = m
        l_s[h, t, :, cs] = l
        d_s[h, t, :, cs] = d

    whole, first, second = slice(0, B), slice(0, half_b), slice(half_b, B)

    def tile_a(h, t, k, v, q, g, r, diagonal):
        if not diagonal:
            stats(h, t, whole, r, [(whole, nt(k, q), nt(v, g))])
            return
        seen = (lax.broadcasted_iota(jnp.int32, (half_b, half_b), 1)
                >= lax.broadcasted_iota(jnp.int32, (half_b, half_b), 0))
        s0, y0 = nt(k[first], q), nt(v[first], g)
        s1, y1 = nt(k[second], q[second]), nt(v[second], g[second])
        stats(h, t, first, r, [(first, jnp.where(seen, s0[:, first], -1e30), y0[:, first])])
        stats(h, t, second, r, [(first, s0[:, second], y0[:, second]), (second, jnp.where(seen, s1, -1e30), y1)])

    def offset(h, b):
        return r_s[h, b, 0:1]

    def own_a(h):
        tile_a(h, 2, kw[0, 0], vw[0, 0], block(h, 0, 1), block(h, 1, 1), offset(h, 1), False)
        tile_a(h, 0, kw[0, 0], vw[0, 0], block(h, 0, 0), block(h, 1, 0), offset(h, 0), True)
        tile_a(h, 1, kw[0, 1], vw[0, 1], block(h, 0, 1), block(h, 1, 1), offset(h, 1), True)

    def src_a(s, h):
        tile_a(h, 1 + 2 * s, kw[s, 0], vw[s, 0], block(h, 0, 1), block(h, 1, 1), offset(h, 1), False)
        tile_a(h, 2 + 2 * s, kw[s, 1], vw[s, 1], mixed(h, 0, s), mixed(h, 1, s),
               pick(early[s], offset(h, 0), offset(h, 1)), False)

    def totals(h):
        hi_tiles = [1, 2] + [1 + 2 * s for s in range(1, WINDOW)]
        ms = [m_s[h, t] for t in range(TILES)]
        m_lo = ms[0]
        m_hi = functools.reduce(jnp.maximum, [ms[t] for t in hi_tiles])
        for s in range(1, WINDOW):
            mx = ms[2 + 2 * s]
            m_lo = jnp.maximum(m_lo, pick(early[s], mx, -3e38))
            m_hi = jnp.maximum(m_hi, pick(early[s], -3e38, mx))
        f = {0: jnp.exp2((ms[0] - m_lo) * C1)}
        for t in hi_tiles:
            f[t] = jnp.exp2((ms[t] - m_hi) * C1)
        l_lo, d_lo = f[0] * l_s[h, 0], f[0] * d_s[h, 0]
        l_hi = sum(f[t] * l_s[h, t] for t in hi_tiles)
        d_hi = sum(f[t] * d_s[h, t] for t in hi_tiles)
        for s in range(1, WINDOW):
            t = 2 + 2 * s
            f[t] = jnp.exp2((ms[t] - pick(early[s], m_lo, m_hi)) * C1)
            a, b = f[t] * l_s[h, t], f[t] * d_s[h, t]
            l_lo += pick(early[s], a, 0.0)
            l_hi += pick(early[s], 0.0, a)
            d_lo += pick(early[s], b, 0.0)
            d_hi += pick(early[s], 0.0, b)
        i_lo, i_hi = 1.0 / l_lo, 1.0 / l_hi
        elo_s[h] = d_lo * i_lo
        ehi_s[h] = d_hi * i_hi
        c_s[h, 0] = f[0] * i_lo
        for t in hi_tiles:
            c_s[h, t] = f[t] * i_hi
        for s in range(1, WINDOW):
            t = 2 + 2 * s
            c_s[h, t] = f[t] * pick(early[s], i_lo, i_hi)

    slot = (0, 1, 2, 1)
    acc[...] = jnp.zeros_like(acc)
    dqt[...] = jnp.zeros_like(dqt)
    core = c % 2

    def relay_if(s, parity):
        @pl.when(core == parity)
        def _():
            relay(s)

    relay(0)
    prep(0)
    middle = 0.5 * (jnp.mean(vw[0, 0].astype(F32), axis=0, keepdims=True)
                    + jnp.mean(vw[0, 1].astype(F32), axis=0, keepdims=True))
    mid[...] = jnp.broadcast_to(middle, (8, D)).astype(BF)
    relay_if(1, 1)
    take_head(0)
    own_a(0)
    relay_if(1, 0)
    prep(1)
    src_a(1, 0)
    relay_if(2, 1)
    take_head(1)
    own_a(1)
    src_a(1, 1)
    relay_if(2, 0)
    prep(2)
    src_a(2, 0)
    src_a(2, 1)
    take_head(2)
    own_a(2)
    src_a(1, 2)
    src_a(2, 2)
    relay(3)
    prep(3)
    for h in range(3):
        src_a(3, h)
    for h in range(3):
        totals(h)

    def weights(h, t, e, rs, cs):
        pn = p_s[h, t, rs, cs].astype(F32) * c_s[h, t, :, cs]
        ds = (pn * (dp_s[h, t, rs, cs].astype(F32) - e[:, cs])).astype(BF)
        return pn.astype(BF), ds

    def tile_b(h, t, e, k_t, q, g):
        p, ds = weights(h, t, e, whole, whole)
        return nn(ds, q), nn(p, g), nn(k_t, ds)

    def src_b(s, hs):
        total = None
        for h in hs:
            k0, v0, q0 = tile_b(h, 1 + 2 * s, ehi_s[h], kt[s, 0], block(h, 0, 1), block(h, 1, 1))
            k1, v1, q1 = tile_b(h, 2 + 2 * s, pick(early[s], elo_s[h], ehi_s[h]), kt[s, 1],
                                mixed(h, 0, s), mixed(h, 1, s))
            dqt[h, 0] += pick(early[s], q1, 0.0)
            dqt[h, 1] += q0 + pick(early[s], 0.0, q1)
            new = (k0, k1, v0, v1)
            total = new if total is None else tuple(a + b for a, b in zip(total, new))
        for i, x in enumerate(total):
            acc[slot[s], i // 2, i % 2] += x

    def partial(s, n):
        unit = SCALE if n == 0 else 1.0
        if s == 0:
            return acc[0, n, 0] * unit, acc[0, n, 1] * unit
        lo, ex = acc[slot[s], n, 0] * unit, acc[slot[s], n, 1] * unit
        return lo + pick(early[s], ex, 0.0), pick(early[s], 0.0, ex)

    def pass_on(s):
        step = WINDOW - 1 - s
        arrived(kv.at[step], kv_send.at[step])
        for n in (1, 0):
            lo, hi = partial(s, n)
            if step > 0:
                arrived(cin.at[step - 1, n], c_recv.at[step - 1, n])
                lo = lo + cin[step - 1, n, 0:B].astype(F32)
                hi = hi + cin[step - 1, n, B:ROWS].astype(F32)
            kv[step, n, 0:B] = lo.astype(BF)
            kv[step, n, B:ROWS] = hi.astype(BF)
            remote(kv.at[step, n], cin.at[step, n], c_send.at[step], c_recv.at[step, n], prv).start()

    def out_rows(src, dst, col, ssem, rsem):
        pltpu.make_async_copy(src.at[rows(hm)], dst.at[:, cols(col)], rsem).start()
        for j in peers:
            remote(src.at[rows(j)], dst.at[:, cols(col)], ssem, rsem, (c, j)).start()

    def diag_b(h, t, e, k_t, q, g):
        p0, ds0 = weights(h, t, e, first, first)
        p1, ds1 = weights(h, t, e, whole, second)
        return ((nn(ds0, q[first]), nn(ds1, q[second])), (nn(p0, g[first]), nn(p1, g[second])),
                (nn(k_t[:, first], ds0), nn(k_t, ds1)))

    def own_b(h):
        k2, v2, q2 = tile_b(h, 2, ehi_s[h], kt[0, 0], block(h, 0, 1), block(h, 1, 1))
        dk0, dv0, q0 = diag_b(h, 0, elo_s[h], kt[0, 0], block(h, 0, 0), block(h, 1, 0))
        dk1, dv1, q1 = diag_b(h, 1, ehi_s[h], kt[0, 1], block(h, 0, 1), block(h, 1, 1))
        for n, full, d0, d1 in ((0, k2, dk0, dk1), (1, v2, dv0, dv1)):
            acc[0, n, 0] += full + d0[1]
            acc[0, n, 0, first] += d0[0]
            acc[0, n, 1] += d1[1]
            acc[0, n, 1, first] += d1[0]
        for cs, a, b in ((first, q0[0], q1[0]), (second, q0[1], q1[1])):
            lo = ((dqt[h, 0, :, cs] + a) * SCALE).T.astype(BF)
            hi = ((dqt[h, 1, :, cs] + b + q2[:, cs]) * SCALE).T.astype(BF)
            qg[h, 0, cs] = pick(low[0], hi, lo)
            qg[h, 0, slice(cs.start + B, cs.stop + B)] = pick(low[0], lo, hi)
        out_rows(qg.at[h, 0], gq, mine * HEADS + h, dq_send.at[0], dq_recv.at[0])

    src_b(3, (0, 1, 2))
    take_head(3)
    own_a(3)
    for s in range(1, WINDOW):
        src_a(s, 3)
    totals(3)
    src_b(3, (3,))
    pass_on(3)
    acc[slot[1]] = jnp.zeros(acc.shape[1:], F32)
    src_b(2, (0,))

    def last_b(h, carry):
        @pl.when(h == 1)
        def _():
            src_b(2, (1, 2, 3))

        @pl.when((h == 1) & (core == 0))
        def _():
            pass_on(2)

        src_b(1, (h,))
        own_b(h)

        @pl.when(h * core == 1)
        def _():
            pass_on(2)

        return carry

    lax.fori_loop(0, HEADS, last_b, 0)
    pass_on(1)

    for n, dst in ((1, gv), (0, gk)):
        lo, hi = partial(0, n)
        arrived(cin.at[WINDOW - 2, n], c_recv.at[WINDOW - 2, n])
        lo = (lo + cin[WINDOW - 2, n, 0:B].astype(F32)).astype(BF)
        hi = (hi + cin[WINDOW - 2, n, B:ROWS].astype(F32)).astype(BF)
        kv[WINDOW - 1, n, 0:B] = pick(low[0], hi, lo)
        kv[WINDOW - 1, n, B:ROWS] = pick(low[0], lo, hi)
        out_rows(kv.at[WINDOW - 1, n], dst, mine, fin_send.at[n], fin_recv.at[n])

    sent = 128 - 128 // KV_HEADS
    for n, ref in enumerate((key, value, query, d_out)):
        arrived(ref.at[0:sent], in_send.at[n])
    for s in range(WINDOW - 1):
        arrived(kv.at[s], c_send.at[s])
    arrived(gq.at[0:sent], dq_send.at[0])
    arrived(gq, dq_recv.at[0])
    for n, ref in ((0, gk), (1, gv)):
        arrived(ref.at[0:sent], fin_send.at[n])
        arrived(ref, fin_recv.at[n])


def land(*refs):
    src, dst, buf, sem_in, sem_out = refs[0:3], refs[3:6], refs[6:9], refs[9], refs[10]
    pieces = []
    for n in (0, 0, 0, 0, 1, 2):
        size = src[n].shape[0] // (4 if n == 0 else 1)
        pieces.append((n, pl.ds(size * len(pieces) if n == 0 else 0, size)))
    for i, (n, rs) in enumerate(pieces):
        pltpu.make_async_copy(src[n].at[rs], buf[n].at[rs], sem_in.at[i]).start()
    for i, (n, rs) in enumerate(pieces):
        pltpu.make_async_copy(src[n].at[rs], buf[n].at[rs], sem_in.at[i]).wait()
        pltpu.make_async_copy(buf[n].at[rs], dst[n].at[rs], sem_out.at[i]).start()
    for i, (n, rs) in enumerate(pieces):
        pltpu.make_async_copy(buf[n].at[rs], dst[n].at[rs], sem_out.at[i]).wait()


def body(query, key, value, d_out, stretch_ids):
    anyspec = pl.BlockSpec(memory_space=pl.ANY)
    dma = pltpu.SemaphoreType.DMA
    stat = pltpu.VMEM((HEADS, TILES, 1, B), F32)
    pair = (2, ROWS, D)
    outs = pl.pallas_call(
        kernel,
        out_shape=tuple(jax.ShapeDtypeStruct(a.shape, BF) for a in (query, key, value)),
        in_specs=[pl.BlockSpec(memory_space=pltpu.SMEM)] + [anyspec] * 4,
        out_specs=(anyspec,) * 3,
        scratch_shapes=[
            pltpu.VMEM((HEADS,) + pair, BF),
            pltpu.VMEM((WINDOW,) + pair, BF),
            pltpu.VMEM((WINDOW, 2, B, D), BF),
            pltpu.VMEM((WINDOW, 2, B, D), BF),
            pltpu.VMEM((WINDOW, 2, D, B), BF),
            pltpu.VMEM((HEADS, TILES, B, B), BF),
            pltpu.VMEM((HEADS, TILES, B, B), BF),
            stat, stat, stat, stat,
            pltpu.VMEM((HEADS, 1, B), F32), pltpu.VMEM((HEADS, 1, B), F32),
            pltpu.VMEM((HEADS, 2, 8, B), F32), pltpu.VMEM((8, D), BF),
            pltpu.VMEM((WINDOW - 1, 2, 2, B, D), F32),
            pltpu.VMEM((HEADS, 2, D, B), F32),
            pltpu.VMEM((WINDOW - 1,) + pair, BF),
            dma((1 + HEADS,)), dma((4,)), dma((WINDOW - 1,)), dma((WINDOW - 1,)),
            dma((1,)), dma((1,)), dma((WINDOW - 1, 2)), dma((WINDOW - 1,)), dma((2,)), dma((2,)),
        ],
        compiler_params=pltpu.CompilerParams(
            collective_id=0, has_side_effects=True, vmem_limit_bytes=67043328),
    )(stretch_ids, query, key, value, d_out)
    shapes = tuple(jax.ShapeDtypeStruct(a.shape, BF) for a in outs)
    return pl.pallas_call(
        land, in_specs=[anyspec] * 3, out_specs=(anyspec,) * 3, out_shape=shapes,
        scratch_shapes=[pltpu.VMEM(a.shape, BF) for a in outs] + [dma((6,)), dma((6,))])(*outs)


def solution(mesh):
    spec = P(("ctx", "head"), None)
    return jax.shard_map(
        body,
        mesh=mesh,
        in_specs=(spec, spec, spec, spec, P()),
        out_specs=(spec, spec, spec),
        check_vma=False,
    )
```

```python
import functools

import jax
import jax.numpy as jnp
from jax import lax
from jax.experimental import pallas as pl
from jax.experimental.pallas import tpu as pltpu
from jax.sharding import PartitionSpec as P

HEADS = 4
KV_HEADS = 8
D = 128
B = 512
ROWS = 2 * B
WINDOW = 4
BF = jnp.bfloat16
F32 = jnp.float32
SCALE = D ** -0.5
LOG2E = 1.4426950408889634
C1 = SCALE * LOG2E
MESH = pl.DeviceIdType.MESH
TILES = 9


def nt(a, b):
    return lax.dot_general(a, b, (((1,), (1,)), ((), ())), preferred_element_type=F32)


def nn(a, b):
    return lax.dot_general(a, b, (((1,), (0,)), ((), ())), preferred_element_type=F32)


def kernel(
    ids, query, key, value, d_out, gq, gk, gv,
    qg, kv, kw, vw, kt, p_s, dp_s, m_s, l_s, d_s, c_s, elo_s, ehi_s, r_s, mid, acc, dqt, cin,
    in_recv, in_send, kv_recv, kv_send, dq_recv, dq_send, c_recv, c_send, fin_recv, fin_send,
):
    c = lax.axis_index("ctx")
    hm = lax.axis_index("head")
    n_ctx = lax.axis_size("ctx")
    half = n_ctx // 2
    flip = c // half
    z, x = hm // 2, hm % 2

    def group_at(device):
        return device + flip * (1 - 2 * (device % 2))

    def ctx_peer(by):
        other = lax.rem(c + by + n_ctx, n_ctx)
        crossed = (other // half - flip) * (other // half - flip)
        return (other, hm + crossed * (1 - 2 * x))

    mine = group_at(hm)
    nxt, prv = ctx_peer(1), ctx_peer(-1)
    peers = []
    for dz, dx in ((1, 0), (3, 0), (0, 1), (2, 0), (1, 1), (3, 1), (2, 1)):
        pz = lax.rem(z + dz, 4)
        px = x + dx * (1 - 2 * x)
        peers.append(pz * 2 + px)

    ranks = [lax.rem(c - s + n_ctx, n_ctx) for s in range(WINDOW)]
    pairs = [(ids[2 * r], ids[2 * r + 1]) for r in ranks]
    low = [a > b for a, b in pairs]
    least = [jnp.minimum(a, b) for a, b in pairs]
    early = [None] + [least[0] > least[s] for s in range(1, WINDOW)]

    barrier = pltpu.get_barrier_semaphore()
    for j in peers:
        pl.semaphore_signal(barrier, inc=1, device_id=(c, j), device_id_type=MESH)
    for other in (nxt, prv):
        pl.semaphore_signal(barrier, inc=1, device_id=other, device_id_type=MESH)
    pl.semaphore_wait(barrier, 9)

    def remote(src, dst, ssem, rsem, dev):
        return pltpu.make_async_remote_copy(
            src_ref=src, dst_ref=dst, send_sem=ssem, recv_sem=rsem, device_id=dev, device_id_type=MESH)

    def cols(index):
        return pl.ds(pl.multiple_of(index * D, D), D)

    def slot_rows(index):
        return index // 4, pl.ds(pl.multiple_of(index % 4 * 128, 128), 128)

    def rows(index):
        return pl.ds(pl.multiple_of(index * 128, 128), 128)

    for n, src in enumerate((key, value)):
        pltpu.make_async_copy(src.at[:, cols(mine)], kv.at[(0, n) + slot_rows(hm)], in_recv.at[0]).start()
        for j in peers:
            remote(src.at[:, cols(group_at(j))], kv.at[(0, n) + slot_rows(hm)], in_send.at[n], in_recv.at[0], (c, j)).start()

    def send_head(h, carry):
        for n, src in enumerate((query, d_out)):
            pltpu.make_async_copy(
                src.at[:, cols(mine * HEADS + h)], qg.at[h, n, rows(hm)], in_recv.at[1 + h]).start()
            for j in peers:
                remote(src.at[:, cols(group_at(j) * HEADS + h)], qg.at[h, n, rows(hm)],
                       in_send.at[2 + n], in_recv.at[1 + h], (c, j)).start()
        return carry

    core = c % 2

    sent = 128 - 128 // KV_HEADS

    def send_heads(parity):
        @pl.when(core == parity)
        def _():
            lax.fori_loop(0, HEADS, send_head, 0)

    send_heads(0)

    def arrived(buf, sem):
        pltpu.make_async_copy(buf, buf, sem).wait()

    def pick(cond, a, b):
        return jnp.where(cond, a, b)

    def relay(s):
        if s == 0:
            arrived(kv.at[0], in_recv.at[0])
        else:
            arrived(kv.at[s], kv_recv.at[s - 1])
        if s < WINDOW - 1:
            remote(kv.at[s], kv.at[s + 1], kv_send.at[s], kv_recv.at[s], nxt).start()

    def prep(s):
        for n, w in ((0, kw), (1, vw)):
            a, b = kv[s, n, 0], kv[s, n, 1]
            lo, hi = pick(low[s], b, a), pick(low[s], a, b)
            w[s, 0] = lo
            w[s, 1] = hi if s == 0 else pick(early[s], lo, hi)
        for b in (0, 1):
            kt[s, b] = kw[s, b].T

    def take_head(h):
        arrived(qg.at[h], in_recv.at[1 + h])
        for n in (0, 1):
            a, b = qg[h, n, 0:B], qg[h, n, B:ROWS]
            qg[h, n, 0:B] = pick(low[0], b, a)
            qg[h, n, B:ROWS] = pick(low[0], a, b)
        for b in (0, 1):
            r_s[h, b] = nt(mid[...], block(h, 1, b))

    def block(h, n, b):
        return qg[h, n, b * B:(b + 1) * B]

    def mixed(h, n, s):
        return pick(early[s], block(h, n, 0), block(h, n, 1))

    half_b = B // 2

    def stats(h, t, cs, r, parts):
        m = functools.reduce(jnp.maximum, [jnp.max(x, axis=0, keepdims=True) for _, x, _ in parts])
        l, d = 0.0, 0.0
        for rs, x, y in parts:
            p = jnp.exp2(x * C1 - m * C1)
            y = y - r[:, cs]
            l = l + jnp.sum(p, axis=0, keepdims=True)
            d = d + jnp.sum(p * y, axis=0, keepdims=True)
            p_s[h, t, rs, cs] = p.astype(BF)
            dp_s[h, t, rs, cs] = y.astype(BF)
        m_s[h, t, :, cs] = m
        l_s[h, t, :, cs] = l
        d_s[h, t, :, cs] = d

    whole, first, second = slice(0, B), slice(0, half_b), slice(half_b, B)

    def tile_a(h, t, k, v, q, g, r, diagonal):
        if not diagonal:
            stats(h, t, whole, r, [(whole, nt(k, q), nt(v, g))])
            return
        seen = (lax.broadcasted_iota(jnp.int32, (half_b, half_b), 1)
                >= lax.broadcasted_iota(jnp.int32, (half_b, half_b), 0))
        s0, y0 = nt(k[first], q), nt(v[first], g)
        s1, y1 = nt(k[second], q[second]), nt(v[second], g[second])
        stats(h, t, first, r, [(first, jnp.where(seen, s0[:, first], -1e30), y0[:, first])])
        stats(h, t, second, r, [(first, s0[:, second], y0[:, second]), (second, jnp.where(seen, s1, -1e30), y1)])

    def offset(h, b):
        return r_s[h, b, 0:1]

    def own_a(h):
        tile_a(h, 2, kw[0, 0], vw[0, 0], block(h, 0, 1), block(h, 1, 1), offset(h, 1), False)
        tile_a(h, 0, kw[0, 0], vw[0, 0], block(h, 0, 0), block(h, 1, 0), offset(h, 0), True)
        tile_a(h, 1, kw[0, 1], vw[0, 1], block(h, 0, 1), block(h, 1, 1), offset(h, 1), True)

    def src_a(s, h):
        tile_a(h, 1 + 2 * s, kw[s, 0], vw[s, 0], block(h, 0, 1), block(h, 1, 1), offset(h, 1), False)
        tile_a(h, 2 + 2 * s, kw[s, 1], vw[s, 1], mixed(h, 0, s), mixed(h, 1, s),
               pick(early[s], offset(h, 0), offset(h, 1)), False)

    def totals(h):
        hi_tiles = [1, 2] + [1 + 2 * s for s in range(1, WINDOW)]
        ms = [m_s[h, t] for t in range(TILES)]
        m_lo = ms[0]
        m_hi = functools.reduce(jnp.maximum, [ms[t] for t in hi_tiles])
        for s in range(1, WINDOW):
            mx = ms[2 + 2 * s]
            m_lo = jnp.maximum(m_lo, pick(early[s], mx, -3e38))
            m_hi = jnp.maximum(m_hi, pick(early[s], -3e38, mx))
        f = {0: jnp.exp2((ms[0] - m_lo) * C1)}
        for t in hi_tiles:
            f[t] = jnp.exp2((ms[t] - m_hi) * C1)
        l_lo, d_lo = f[0] * l_s[h, 0], f[0] * d_s[h, 0]
        l_hi = sum(f[t] * l_s[h, t] for t in hi_tiles)
        d_hi = sum(f[t] * d_s[h, t] for t in hi_tiles)
        for s in range(1, WINDOW):
            t = 2 + 2 * s
            f[t] = jnp.exp2((ms[t] - pick(early[s], m_lo, m_hi)) * C1)
            a, b = f[t] * l_s[h, t], f[t] * d_s[h, t]
            l_lo += pick(early[s], a, 0.0)
            l_hi += pick(early[s], 0.0, a)
            d_lo += pick(early[s], b, 0.0)
            d_hi += pick(early[s], 0.0, b)
        i_lo, i_hi = 1.0 / l_lo, 1.0 / l_hi
        elo_s[h] = d_lo * i_lo
        ehi_s[h] = d_hi * i_hi
        c_s[h, 0] = f[0] * i_lo
        for t in hi_tiles:
            c_s[h, t] = f[t] * i_hi
        for s in range(1, WINDOW):
            t = 2 + 2 * s
            c_s[h, t] = f[t] * pick(early[s], i_lo, i_hi)

    slot = (0, 1, 2, 1)
    acc[...] = jnp.zeros_like(acc)
    dqt[...] = jnp.zeros_like(dqt)
    def relay_if(s, parity):
        @pl.when(core == parity)
        def _():
            relay(s)

    for n, ref in enumerate((key, value)):
        arrived(ref.at[0:sent], in_send.at[n])
    send_heads(1)
    relay(0)
    prep(0)
    middle = 0.5 * (jnp.mean(vw[0, 0].astype(F32), axis=0, keepdims=True)
                    + jnp.mean(vw[0, 1].astype(F32), axis=0, keepdims=True))
    mid[...] = jnp.broadcast_to(middle, (8, D)).astype(BF)
    relay_if(1, 1)
    take_head(0)
    own_a(0)
    relay_if(1, 0)
    prep(1)
    src_a(1, 0)
    relay_if(2, 1)
    take_head(1)
    own_a(1)
    src_a(1, 1)
    relay_if(2, 0)
    prep(2)
    src_a(2, 0)
    src_a(2, 1)
    take_head(2)
    own_a(2)
    src_a(1, 2)
    src_a(2, 2)
    relay(3)
    prep(3)
    for h in range(3):
        src_a(3, h)
    for h in range(3):
        totals(h)

    def weights(h, t, e, rs, cs):
        pn = p_s[h, t, rs, cs].astype(F32) * c_s[h, t, :, cs]
        ds = (pn * (dp_s[h, t, rs, cs].astype(F32) - e[:, cs])).astype(BF)
        return pn.astype(BF), ds

    def tile_b(h, t, e, k_t, q, g):
        p, ds = weights(h, t, e, whole, whole)
        return nn(ds, q), nn(p, g), nn(k_t, ds)

    def src_b(s, hs):
        total = None
        for h in hs:
            k0, v0, q0 = tile_b(h, 1 + 2 * s, ehi_s[h], kt[s, 0], block(h, 0, 1), block(h, 1, 1))
            k1, v1, q1 = tile_b(h, 2 + 2 * s, pick(early[s], elo_s[h], ehi_s[h]), kt[s, 1],
                                mixed(h, 0, s), mixed(h, 1, s))
            dqt[h, 0] += pick(early[s], q1, 0.0)
            dqt[h, 1] += q0 + pick(early[s], 0.0, q1)
            new = (k0, k1, v0, v1)
            total = new if total is None else tuple(a + b for a, b in zip(total, new))
        for i, x in enumerate(total):
            acc[slot[s], i // 2, i % 2] += x

    quarters = [(n, hf, slice(hf * half_b, (hf + 1) * half_b)) for n in (1, 0) for hf in (0, 1)]

    def partial(s, n, rs):
        unit = SCALE if n == 0 else 1.0
        a, b = acc[slot[s], n, 0, rs] * unit, acc[slot[s], n, 1, rs] * unit
        if s == 0:
            return a, b
        return a + pick(early[s], b, 0.0), pick(early[s], 0.0, b)

    def summed(s, n, hf, rs):
        step = WINDOW - 1 - s
        lo, hi = partial(s, n, rs)
        if step > 0:
            arrived(cin.at[step - 1, n, :, rs], c_recv.at[step - 1, n, hf])
            lo = lo + cin[step - 1, n, 0, rs].astype(F32)
            hi = hi + cin[step - 1, n, 1, rs].astype(F32)
        return lo.astype(BF), hi.astype(BF)

    def pass_on(s):
        step = WINDOW - 1 - s
        arrived(kv.at[step], kv_send.at[step])
        for n, hf, rs in quarters:
            kv[step, n, 0, rs], kv[step, n, 1, rs] = summed(s, n, hf, rs)
            remote(kv.at[step, n, :, rs], cin.at[step, n, :, rs], c_send.at[step], c_recv.at[step, n, hf], prv).start()

    def out_rows(src, dst, col, ssem, rsem):
        pltpu.make_async_copy(src.at[rows(hm)], dst.at[:, cols(col)], rsem).start()
        for j in peers:
            remote(src.at[rows(j)], dst.at[:, cols(col)], ssem, rsem, (c, j)).start()

    def diag_b(h, t, e, k_t, q, g):
        p0, ds0 = weights(h, t, e, first, first)
        p1, ds1 = weights(h, t, e, whole, second)
        return ((nn(ds0, q[first]), nn(ds1, q[second])), (nn(p0, g[first]), nn(p1, g[second])),
                (nn(k_t[:, first], ds0), nn(k_t, ds1)))

    def own_b(h):
        k2, v2, q2 = tile_b(h, 2, ehi_s[h], kt[0, 0], block(h, 0, 1), block(h, 1, 1))
        dk0, dv0, q0 = diag_b(h, 0, elo_s[h], kt[0, 0], block(h, 0, 0), block(h, 1, 0))
        dk1, dv1, q1 = diag_b(h, 1, ehi_s[h], kt[0, 1], block(h, 0, 1), block(h, 1, 1))
        for n, full, d0, d1 in ((0, k2, dk0, dk1), (1, v2, dv0, dv1)):
            acc[0, n, 0] += full + d0[1]
            acc[0, n, 0, first] += d0[0]
            acc[0, n, 1] += d1[1]
            acc[0, n, 1, first] += d1[0]
        for cs, a, b in ((first, q0[0], q1[0]), (second, q0[1], q1[1])):
            lo = ((dqt[h, 0, :, cs] + a) * SCALE).T.astype(BF)
            hi = ((dqt[h, 1, :, cs] + b + q2[:, cs]) * SCALE).T.astype(BF)
            qg[h, 0, cs] = pick(low[0], hi, lo)
            qg[h, 0, slice(cs.start + B, cs.stop + B)] = pick(low[0], lo, hi)
        out_rows(qg.at[h, 0], gq, mine * HEADS + h, dq_send.at[0], dq_recv.at[0])

    take_head(3)
    src_b(3, (0, 1, 2))
    own_a(3)
    for s in range(1, WINDOW):
        src_a(s, 3)
    totals(3)
    src_b(3, (3,))
    pass_on(3)
    acc[slot[1]] = jnp.zeros(acc.shape[1:], F32)
    src_b(2, (0,))

    def last_b(h, carry):
        @pl.when(h == 1)
        def _():
            src_b(2, (1, 2, 3))

        @pl.when((h == 1) & (core == 0))
        def _():
            pass_on(2)

        src_b(1, (h,))
        own_b(h)

        @pl.when(h * core == 1)
        def _():
            pass_on(2)

        return carry

    def pass_on_if(s, parity):
        @pl.when(core == parity)
        def _():
            pass_on(s)

    lax.fori_loop(0, HEADS - 1, last_b, 0)
    src_b(1, (HEADS - 1,))
    pass_on_if(1, 0)
    own_b(HEADS - 1)
    pass_on_if(1, 1)

    for n, hf, rs in quarters:
        lo, hi = summed(0, n, hf, rs)
        kv[WINDOW - 1, n, 0, rs] = pick(low[0], hi, lo)
        kv[WINDOW - 1, n, 1, rs] = pick(low[0], lo, hi)
        dst = (gk, gv)[n].at[:, cols(mine)]

        @pl.when(hm % 4 // 2 == hf)
        def _():
            pltpu.make_async_copy(kv.at[(WINDOW - 1, n) + slot_rows(hm)], dst, fin_recv.at[n]).start()

        for j in peers:
            @pl.when(j % 4 // 2 == hf)
            def _():
                remote(kv.at[(WINDOW - 1, n) + slot_rows(j)], dst, fin_send.at[n], fin_recv.at[n], (c, j)).start()

    for n, ref in ((2, query), (3, d_out)):
        arrived(ref.at[0:sent], in_send.at[n])
    for s in range(WINDOW - 1):
        arrived(kv.at[s], c_send.at[s])
    arrived(gq.at[0:sent], dq_send.at[0])
    arrived(gq, dq_recv.at[0])
    for n, ref in ((0, gk), (1, gv)):
        arrived(ref.at[0:sent], fin_send.at[n])
        arrived(ref, fin_recv.at[n])


def land(*refs):
    src, dst, buf, sem_in, sem_out = refs[0:3], refs[3:6], refs[6:9], refs[9], refs[10]
    pieces = []
    for n in (0, 0, 0, 0, 1, 2):
        size = src[n].shape[0] // (4 if n == 0 else 1)
        pieces.append((n, pl.ds(size * len(pieces) if n == 0 else 0, size)))
    for i, (n, rs) in enumerate(pieces):
        pltpu.make_async_copy(src[n].at[rs], buf[n].at[rs], sem_in.at[i]).start()
    for i, (n, rs) in enumerate(pieces):
        pltpu.make_async_copy(src[n].at[rs], buf[n].at[rs], sem_in.at[i]).wait()
        pltpu.make_async_copy(buf[n].at[rs], dst[n].at[rs], sem_out.at[i]).start()
    for i, (n, rs) in enumerate(pieces):
        pltpu.make_async_copy(buf[n].at[rs], dst[n].at[rs], sem_out.at[i]).wait()


def body(query, key, value, d_out, stretch_ids):
    anyspec = pl.BlockSpec(memory_space=pl.ANY)
    dma = pltpu.SemaphoreType.DMA
    stat = pltpu.VMEM((HEADS, TILES, 1, B), F32)
    pair = (2, ROWS, D)
    slots = (2, 2, B, D)
    outs = pl.pallas_call(
        kernel,
        out_shape=tuple(jax.ShapeDtypeStruct(a.shape, BF) for a in (query, key, value)),
        in_specs=[pl.BlockSpec(memory_space=pltpu.SMEM)] + [anyspec] * 4,
        out_specs=(anyspec,) * 3,
        scratch_shapes=[
            pltpu.VMEM((HEADS,) + pair, BF),
            pltpu.VMEM((WINDOW,) + slots, BF),
            pltpu.VMEM((WINDOW, 2, B, D), BF),
            pltpu.VMEM((WINDOW, 2, B, D), BF),
            pltpu.VMEM((WINDOW, 2, D, B), BF),
            pltpu.VMEM((HEADS, TILES, B, B), BF),
            pltpu.VMEM((HEADS, TILES, B, B), BF),
            stat, stat, stat, stat,
            pltpu.VMEM((HEADS, 1, B), F32), pltpu.VMEM((HEADS, 1, B), F32),
            pltpu.VMEM((HEADS, 2, 8, B), F32), pltpu.VMEM((8, D), BF),
            pltpu.VMEM((WINDOW - 1, 2, 2, B, D), F32),
            pltpu.VMEM((HEADS, 2, D, B), F32),
            pltpu.VMEM((WINDOW - 1,) + slots, BF),
            dma((1 + HEADS,)), dma((4,)), dma((WINDOW - 1,)), dma((WINDOW - 1,)),
            dma((1,)), dma((1,)), dma((WINDOW - 1, 2, 2)), dma((WINDOW - 1,)), dma((2,)), dma((2,)),
        ],
        compiler_params=pltpu.CompilerParams(
            collective_id=0, has_side_effects=True, vmem_limit_bytes=67043328),
    )(stretch_ids, query, key, value, d_out)
    shapes = tuple(jax.ShapeDtypeStruct(a.shape, BF) for a in outs)
    return pl.pallas_call(
        land, in_specs=[anyspec] * 3, out_specs=(anyspec,) * 3, out_shape=shapes,
        scratch_shapes=[pltpu.VMEM(a.shape, BF) for a in outs] + [dma((6,)), dma((6,))])(*outs)


def solution(mesh):
    spec = P(("ctx", "head"), None)
    return jax.shard_map(
        body,
        mesh=mesh,
        in_specs=(spec, spec, spec, spec, P()),
        out_specs=(spec, spec, spec),
        check_vma=False,
    )
```

```python
import functools

import jax
import jax.numpy as jnp
from jax import lax
from jax.experimental import pallas as pl
from jax.experimental.pallas import tpu as pltpu
from jax.sharding import PartitionSpec as P

HEADS = 4
KV_HEADS = 8
D = 128
B = 512
ROWS = 2 * B
WINDOW = 4
BF = jnp.bfloat16
F32 = jnp.float32
SCALE = D ** -0.5
LOG2E = 1.4426950408889634
C1 = SCALE * LOG2E
MESH = pl.DeviceIdType.MESH
TILES = 9


def nt(a, b):
    return lax.dot_general(a, b, (((1,), (1,)), ((), ())), preferred_element_type=F32)


def nn(a, b):
    return lax.dot_general(a, b, (((1,), (0,)), ((), ())), preferred_element_type=F32)


def kernel(
    ids, query, key, value, d_out, gq, gk, gv,
    qg, kv, kw, vw, kt, p_s, dp_s, m_s, l_s, d_s, c_s, elo_s, ehi_s, r_s, mid, acc, dqt, cin,
    in_recv, in_send, kv_recv, kv_send, dq_recv, dq_send, c_recv, c_send, fin_recv, fin_send,
):
    c = lax.axis_index("ctx")
    hm = lax.axis_index("head")
    n_ctx = lax.axis_size("ctx")
    half = n_ctx // 2
    flip = c // half
    z, x = hm // 2, hm % 2

    def group_at(device):
        return device + flip * (1 - 2 * (device % 2))

    def ctx_peer(by):
        other = lax.rem(c + by + n_ctx, n_ctx)
        crossed = (other // half - flip) * (other // half - flip)
        return (other, hm + crossed * (1 - 2 * x))

    mine = group_at(hm)
    nxt, prv = ctx_peer(1), ctx_peer(-1)
    peers = []
    for dz, dx in ((1, 0), (3, 0), (0, 1), (2, 0), (1, 1), (3, 1), (2, 1)):
        pz = lax.rem(z + dz, 4)
        px = x + dx * (1 - 2 * x)
        peers.append(pz * 2 + px)

    ranks = [lax.rem(c - s + n_ctx, n_ctx) for s in range(WINDOW)]
    pairs = [(ids[2 * r], ids[2 * r + 1]) for r in ranks]
    low = [a > b for a, b in pairs]
    least = [jnp.minimum(a, b) for a, b in pairs]
    early = [None] + [least[0] > least[s] for s in range(1, WINDOW)]

    barrier = pltpu.get_barrier_semaphore()
    for j in peers:
        pl.semaphore_signal(barrier, inc=1, device_id=(c, j), device_id_type=MESH)
    for other in (nxt, prv):
        pl.semaphore_signal(barrier, inc=1, device_id=other, device_id_type=MESH)
    pl.semaphore_wait(barrier, 9)

    def remote(src, dst, ssem, rsem, dev):
        return pltpu.make_async_remote_copy(
            src_ref=src, dst_ref=dst, send_sem=ssem, recv_sem=rsem, device_id=dev, device_id_type=MESH)

    def cols(index):
        return pl.ds(pl.multiple_of(index * D, D), D)

    def slot_rows(index):
        return index // 4, pl.ds(pl.multiple_of(index % 4 * 128, 128), 128)

    def rows(index):
        return pl.ds(pl.multiple_of(index * 128, 128), 128)

    for n, src in enumerate((key, value)):
        pltpu.make_async_copy(src.at[:, cols(mine)], kv.at[(0, n) + slot_rows(hm)], in_recv.at[0]).start()
        for j in peers:
            remote(src.at[:, cols(group_at(j))], kv.at[(0, n) + slot_rows(hm)], in_send.at[n], in_recv.at[0], (c, j)).start()

    def send_head(h, carry):
        for n, src in enumerate((query, d_out)):
            pltpu.make_async_copy(
                src.at[:, cols(mine * HEADS + h)], qg.at[h, n, rows(hm)], in_recv.at[1 + h]).start()
            for j in peers:
                remote(src.at[:, cols(group_at(j) * HEADS + h)], qg.at[h, n, rows(hm)],
                       in_send.at[2 + n], in_recv.at[1 + h], (c, j)).start()
        return carry

    core = c % 2

    sent = 128 - 128 // KV_HEADS

    def send_heads(parity):
        @pl.when(core == parity)
        def _():
            lax.fori_loop(0, HEADS, send_head, 0)

    send_heads(0)

    def arrived(buf, sem):
        pltpu.make_async_copy(buf, buf, sem).wait()

    def pick(cond, a, b):
        return jnp.where(cond, a, b)

    def relay(s):
        if s == 0:
            arrived(kv.at[0], in_recv.at[0])
        else:
            arrived(kv.at[s], kv_recv.at[s - 1])
        if s < WINDOW - 1:
            remote(kv.at[s], kv.at[s + 1], kv_send.at[s], kv_recv.at[s], nxt).start()

    def prep(s):
        for n, w in ((0, kw), (1, vw)):
            a, b = kv[s, n, 0], kv[s, n, 1]
            lo, hi = pick(low[s], b, a), pick(low[s], a, b)
            w[s, 0] = lo
            w[s, 1] = hi if s == 0 else pick(early[s], lo, hi)
        for b in (0, 1):
            kt[s, b] = kw[s, b].T

    def take_head(h):
        arrived(qg.at[h], in_recv.at[1 + h])
        for n in (0, 1):
            a, b = qg[h, n, 0:B], qg[h, n, B:ROWS]
            qg[h, n, 0:B] = pick(low[0], b, a)
            qg[h, n, B:ROWS] = pick(low[0], a, b)
        for b in (0, 1):
            r_s[h, b] = nt(mid[...], block(h, 1, b))

    def block(h, n, b):
        return qg[h, n, b * B:(b + 1) * B]

    def mixed(h, n, s):
        return pick(early[s], block(h, n, 0), block(h, n, 1))

    half_b = B // 2

    def stats(h, t, cs, r, parts):
        m = functools.reduce(jnp.maximum, [jnp.max(x, axis=0, keepdims=True) for _, x, _ in parts])
        l, d = 0.0, 0.0
        for rs, x, y in parts:
            p = jnp.exp2(x * C1 - m * C1)
            y = y - r[:, cs]
            l = l + jnp.sum(p, axis=0, keepdims=True)
            d = d + jnp.sum(p * y, axis=0, keepdims=True)
            p_s[h, t, rs, cs] = p.astype(BF)
            dp_s[h, t, rs, cs] = y.astype(BF)
        m_s[h, t, :, cs] = m
        l_s[h, t, :, cs] = l
        d_s[h, t, :, cs] = d

    whole, first, second = slice(0, B), slice(0, half_b), slice(half_b, B)

    def tile_a(h, t, k, v, q, g, r, diagonal):
        if not diagonal:
            stats(h, t, whole, r, [(whole, nt(k, q), nt(v, g))])
            return
        seen = (lax.broadcasted_iota(jnp.int32, (half_b, half_b), 1)
                >= lax.broadcasted_iota(jnp.int32, (half_b, half_b), 0))
        s0, y0 = nt(k[first], q), nt(v[first], g)
        s1, y1 = nt(k[second], q[second]), nt(v[second], g[second])
        stats(h, t, first, r, [(first, jnp.where(seen, s0[:, first], -1e30), y0[:, first])])
        stats(h, t, second, r, [(first, s0[:, second], y0[:, second]), (second, jnp.where(seen, s1, -1e30), y1)])

    def offset(h, b):
        return r_s[h, b, 0:1]

    def own_a(h):
        tile_a(h, 2, kw[0, 0], vw[0, 0], block(h, 0, 1), block(h, 1, 1), offset(h, 1), False)
        tile_a(h, 0, kw[0, 0], vw[0, 0], block(h, 0, 0), block(h, 1, 0), offset(h, 0), True)
        tile_a(h, 1, kw[0, 1], vw[0, 1], block(h, 0, 1), block(h, 1, 1), offset(h, 1), True)

    def src_a(s, h):
        tile_a(h, 1 + 2 * s, kw[s, 0], vw[s, 0], block(h, 0, 1), block(h, 1, 1), offset(h, 1), False)
        tile_a(h, 2 + 2 * s, kw[s, 1], vw[s, 1], mixed(h, 0, s), mixed(h, 1, s),
               pick(early[s], offset(h, 0), offset(h, 1)), False)

    def totals(h):
        hi_tiles = [1, 2] + [1 + 2 * s for s in range(1, WINDOW)]
        ms = [m_s[h, t] for t in range(TILES)]
        m_lo = ms[0]
        m_hi = functools.reduce(jnp.maximum, [ms[t] for t in hi_tiles])
        for s in range(1, WINDOW):
            mx = ms[2 + 2 * s]
            m_lo = jnp.maximum(m_lo, pick(early[s], mx, -3e38))
            m_hi = jnp.maximum(m_hi, pick(early[s], -3e38, mx))
        f = {0: jnp.exp2((ms[0] - m_lo) * C1)}
        for t in hi_tiles:
            f[t] = jnp.exp2((ms[t] - m_hi) * C1)
        l_lo, d_lo = f[0] * l_s[h, 0], f[0] * d_s[h, 0]
        l_hi = sum(f[t] * l_s[h, t] for t in hi_tiles)
        d_hi = sum(f[t] * d_s[h, t] for t in hi_tiles)
        for s in range(1, WINDOW):
            t = 2 + 2 * s
            f[t] = jnp.exp2((ms[t] - pick(early[s], m_lo, m_hi)) * C1)
            a, b = f[t] * l_s[h, t], f[t] * d_s[h, t]
            l_lo += pick(early[s], a, 0.0)
            l_hi += pick(early[s], 0.0, a)
            d_lo += pick(early[s], b, 0.0)
            d_hi += pick(early[s], 0.0, b)
        i_lo, i_hi = 1.0 / l_lo, 1.0 / l_hi
        elo_s[h] = d_lo * i_lo
        ehi_s[h] = d_hi * i_hi
        c_s[h, 0] = f[0] * i_lo
        for t in hi_tiles:
            c_s[h, t] = f[t] * i_hi
        for s in range(1, WINDOW):
            t = 2 + 2 * s
            c_s[h, t] = f[t] * pick(early[s], i_lo, i_hi)

    slot = (0, 1, 2, 1)
    acc[...] = jnp.zeros_like(acc)
    dqt[...] = jnp.zeros_like(dqt)
    def relay_if(s, parity):
        @pl.when(core == parity)
        def _():
            relay(s)

    for n, ref in enumerate((key, value)):
        arrived(ref.at[0:sent], in_send.at[n])
    send_heads(1)
    relay(0)
    prep(0)
    middle = 0.5 * (jnp.mean(vw[0, 0].astype(F32), axis=0, keepdims=True)
                    + jnp.mean(vw[0, 1].astype(F32), axis=0, keepdims=True))
    mid[...] = jnp.broadcast_to(middle, (8, D)).astype(BF)
    relay_if(1, 1)
    take_head(0)
    own_a(0)
    relay_if(1, 0)
    prep(1)
    src_a(1, 0)
    relay_if(2, 1)
    take_head(1)
    own_a(1)
    src_a(1, 1)
    relay_if(2, 0)
    prep(2)
    src_a(2, 0)
    src_a(2, 1)
    take_head(2)
    own_a(2)
    src_a(1, 2)
    src_a(2, 2)
    relay(3)
    prep(3)
    for h in range(3):
        src_a(3, h)
    for h in range(3):
        totals(h)

    def weights(h, t, e, rs, cs):
        pn = p_s[h, t, rs, cs].astype(F32) * c_s[h, t, :, cs]
        ds = (pn * (dp_s[h, t, rs, cs].astype(F32) - e[:, cs])).astype(BF)
        return pn.astype(BF), ds

    def tile_b(h, t, e, k_t, q, g):
        p, ds = weights(h, t, e, whole, whole)
        return nn(ds, q), nn(p, g), nn(k_t, ds)

    def src_b(s, hs):
        total = None
        for h in hs:
            k0, v0, q0 = tile_b(h, 1 + 2 * s, ehi_s[h], kt[s, 0], block(h, 0, 1), block(h, 1, 1))
            k1, v1, q1 = tile_b(h, 2 + 2 * s, pick(early[s], elo_s[h], ehi_s[h]), kt[s, 1],
                                mixed(h, 0, s), mixed(h, 1, s))
            dqt[h, 0] += pick(early[s], q1, 0.0)
            dqt[h, 1] += q0 + pick(early[s], 0.0, q1)
            new = (k0, k1, v0, v1)
            total = new if total is None else tuple(a + b for a, b in zip(total, new))
        for i, x in enumerate(total):
            acc[slot[s], i // 2, i % 2] += x

    quarters = [(n, hf, slice(hf * half_b, (hf + 1) * half_b)) for n in (1, 0) for hf in (0, 1)]

    def partial(s, n, rs):
        unit = SCALE if n == 0 else 1.0
        a, b = acc[slot[s], n, 0, rs] * unit, acc[slot[s], n, 1, rs] * unit
        if s == 0:
            return a, b
        return a + pick(early[s], b, 0.0), pick(early[s], 0.0, b)

    def summed(s, n, hf, rs):
        step = WINDOW - 1 - s
        lo, hi = partial(s, n, rs)
        if step > 0:
            arrived(cin.at[step - 1, n, :, rs], c_recv.at[step - 1, n, hf])
            lo = lo + cin[step - 1, n, 0, rs].astype(F32)
            hi = hi + cin[step - 1, n, 1, rs].astype(F32)
        return lo.astype(BF), hi.astype(BF)

    def pass_on(s):
        step = WINDOW - 1 - s
        arrived(kv.at[step], kv_send.at[step])
        for n, hf, rs in quarters:
            kv[step, n, 0, rs], kv[step, n, 1, rs] = summed(s, n, hf, rs)
            remote(kv.at[step, n, :, rs], cin.at[step, n, :, rs], c_send.at[step], c_recv.at[step, n, hf], prv).start()

    def out_rows(src, dst, col, ssem, rsem):
        pltpu.make_async_copy(src.at[rows(hm)], dst.at[:, cols(col)], rsem).start()
        for j in peers:
            remote(src.at[rows(j)], dst.at[:, cols(col)], ssem, rsem, (c, j)).start()

    def diag_b(h, t, e, k_t, q, g):
        p0, ds0 = weights(h, t, e, first, first)
        p1, ds1 = weights(h, t, e, whole, second)
        return ((nn(ds0, q[first]), nn(ds1, q[second])), (nn(p0, g[first]), nn(p1, g[second])),
                (nn(k_t[:, first], ds0), nn(k_t, ds1)))

    def own_b(h):
        k2, v2, q2 = tile_b(h, 2, ehi_s[h], kt[0, 0], block(h, 0, 1), block(h, 1, 1))
        dk0, dv0, q0 = diag_b(h, 0, elo_s[h], kt[0, 0], block(h, 0, 0), block(h, 1, 0))
        dk1, dv1, q1 = diag_b(h, 1, ehi_s[h], kt[0, 1], block(h, 0, 1), block(h, 1, 1))
        for n, full, d0, d1 in ((0, k2, dk0, dk1), (1, v2, dv0, dv1)):
            acc[0, n, 0] += full + d0[1]
            acc[0, n, 0, first] += d0[0]
            acc[0, n, 1] += d1[1]
            acc[0, n, 1, first] += d1[0]
        for cs, a, b in ((first, q0[0], q1[0]), (second, q0[1], q1[1])):
            lo = ((dqt[h, 0, :, cs] + a) * SCALE).T.astype(BF)
            hi = ((dqt[h, 1, :, cs] + b + q2[:, cs]) * SCALE).T.astype(BF)
            qg[h, 0, cs] = pick(low[0], hi, lo)
            qg[h, 0, slice(cs.start + B, cs.stop + B)] = pick(low[0], lo, hi)
        out_rows(qg.at[h, 0], gq, mine * HEADS + h, dq_send.at[0], dq_recv.at[0])

    take_head(3)
    src_b(3, (0, 1, 2))
    own_a(3)
    for s in range(1, WINDOW):
        src_a(s, 3)
    totals(3)
    src_b(3, (3,))
    pass_on(3)
    acc[slot[1]] = jnp.zeros(acc.shape[1:], F32)
    src_b(2, (0, 1, 2, 3))

    def last_b(h, carry):
        @pl.when((h == 1) & (core == 0))
        def _():
            pass_on(2)

        src_b(1, (h,))
        own_b(h)

        @pl.when(h * core == 1)
        def _():
            pass_on(2)

        return carry

    def pass_on_if(s, parity):
        @pl.when(core == parity)
        def _():
            pass_on(s)

    lax.fori_loop(0, HEADS - 1, last_b, 0)
    src_b(1, (HEADS - 1,))
    pass_on_if(1, 0)
    own_b(HEADS - 1)
    pass_on_if(1, 1)

    for n, hf, rs in quarters:
        lo, hi = summed(0, n, hf, rs)
        kv[WINDOW - 1, n, 0, rs] = pick(low[0], hi, lo)
        kv[WINDOW - 1, n, 1, rs] = pick(low[0], lo, hi)
        dst = (gk, gv)[n].at[:, cols(mine)]

        @pl.when(hm % 4 // 2 == hf)
        def _():
            pltpu.make_async_copy(kv.at[(WINDOW - 1, n) + slot_rows(hm)], dst, fin_recv.at[n]).start()

        for j in peers:
            @pl.when(j % 4 // 2 == hf)
            def _():
                remote(kv.at[(WINDOW - 1, n) + slot_rows(j)], dst, fin_send.at[n], fin_recv.at[n], (c, j)).start()

    for n, ref in ((2, query), (3, d_out)):
        arrived(ref.at[0:sent], in_send.at[n])
    for s in range(WINDOW - 1):
        arrived(kv.at[s], c_send.at[s])
    arrived(gq.at[0:sent], dq_send.at[0])
    arrived(gq, dq_recv.at[0])
    for n, ref in ((0, gk), (1, gv)):
        arrived(ref.at[0:sent], fin_send.at[n])
        arrived(ref, fin_recv.at[n])


def land(*refs):
    src, dst, buf, sem_in, sem_out = refs[0:3], refs[3:6], refs[6:9], refs[9], refs[10]
    pieces = []
    for n in (0, 0, 0, 0, 1, 2):
        size = src[n].shape[0] // (4 if n == 0 else 1)
        pieces.append((n, pl.ds(size * len(pieces) if n == 0 else 0, size)))
    for i, (n, rs) in enumerate(pieces):
        pltpu.make_async_copy(src[n].at[rs], buf[n].at[rs], sem_in.at[i]).start()
    for i, (n, rs) in enumerate(pieces):
        pltpu.make_async_copy(src[n].at[rs], buf[n].at[rs], sem_in.at[i]).wait()
        pltpu.make_async_copy(buf[n].at[rs], dst[n].at[rs], sem_out.at[i]).start()
    for i, (n, rs) in enumerate(pieces):
        pltpu.make_async_copy(buf[n].at[rs], dst[n].at[rs], sem_out.at[i]).wait()


def body(query, key, value, d_out, stretch_ids):
    anyspec = pl.BlockSpec(memory_space=pl.ANY)
    dma = pltpu.SemaphoreType.DMA
    stat = pltpu.VMEM((HEADS, TILES, 1, B), F32)
    pair = (2, ROWS, D)
    slots = (2, 2, B, D)
    outs = pl.pallas_call(
        kernel,
        out_shape=tuple(jax.ShapeDtypeStruct(a.shape, BF) for a in (query, key, value)),
        in_specs=[pl.BlockSpec(memory_space=pltpu.SMEM)] + [anyspec] * 4,
        out_specs=(anyspec,) * 3,
        scratch_shapes=[
            pltpu.VMEM((HEADS,) + pair, BF),
            pltpu.VMEM((WINDOW,) + slots, BF),
            pltpu.VMEM((WINDOW, 2, B, D), BF),
            pltpu.VMEM((WINDOW, 2, B, D), BF),
            pltpu.VMEM((WINDOW, 2, D, B), BF),
            pltpu.VMEM((HEADS, TILES, B, B), BF),
            pltpu.VMEM((HEADS, TILES, B, B), BF),
            stat, stat, stat, stat,
            pltpu.VMEM((HEADS, 1, B), F32), pltpu.VMEM((HEADS, 1, B), F32),
            pltpu.VMEM((HEADS, 2, 8, B), F32), pltpu.VMEM((8, D), BF),
            pltpu.VMEM((WINDOW - 1, 2, 2, B, D), F32),
            pltpu.VMEM((HEADS, 2, D, B), F32),
            pltpu.VMEM((WINDOW - 1,) + slots, BF),
            dma((1 + HEADS,)), dma((4,)), dma((WINDOW - 1,)), dma((WINDOW - 1,)),
            dma((1,)), dma((1,)), dma((WINDOW - 1, 2, 2)), dma((WINDOW - 1,)), dma((2,)), dma((2,)),
        ],
        compiler_params=pltpu.CompilerParams(
            collective_id=0, has_side_effects=True, vmem_limit_bytes=67043328),
    )(stretch_ids, query, key, value, d_out)
    shapes = tuple(jax.ShapeDtypeStruct(a.shape, BF) for a in outs)
    return pl.pallas_call(
        land, in_specs=[anyspec] * 3, out_specs=(anyspec,) * 3, out_shape=shapes,
        scratch_shapes=[pltpu.VMEM(a.shape, BF) for a in outs] + [dma((6,)), dma((6,))])(*outs)


def solution(mesh):
    spec = P(("ctx", "head"), None)
    return jax.shard_map(
        body,
        mesh=mesh,
        in_specs=(spec, spec, spec, spec, P()),
        out_specs=(spec, spec, spec),
        check_vma=False,
    )
```
